32 devices in a mesh: qrow: 4 (over y, x), kcol: 8 (over z, core).
Axes of the slice: x: 2, y: 2, z: 4, core: 2. Of those that a mesh axis runs over, the one named last changes fastest.
Arguments:
- query: bfloat16 [4096, 1024], P('kcol', 'qrow'), may hold values from -6 to 6
- key: bfloat16 [4096, 256], P(('kcol', 'qrow')), may hold values from -6 to 6
- value: bfloat16 [4096, 256], P(('kcol', 'qrow')), may hold values from -6 to 6
- output: bfloat16 [4096, 1024], P('kcol', 'qrow'), may hold values from -6 to 6
- grad_out: bfloat16 [4096, 1024], P('kcol', 'qrow'), may hold values from -6 to 6
- lse: float32 [16, 4096], P('qrow', 'kcol'), may hold values from 2 to 5
- doc_ids: int32 [4096], replicated, may hold values from 0 to 7, never falling along the last dimension, each value on 1 to 3072 neighbouring positions
Outputs:
- grad_query: float32 [4096, 1024], P('kcol', 'qrow')
- grad_key: float32 [4096, 256], P(('kcol', 'qrow'))
- grad_value: float32 [4096, 256], P(('kcol', 'qrow'))
The draws below stay inside these ranges and needn't reach their ends.
Inputs may be any that keep to these rules, and one draw needn't show every extreme that they name: `doc_ids`: document ids never fall along the sequence; no document is longer than 4096 // 2 + 2 * (512) tokens.
All inputs are finite; a program needn't handle non-finite values.
Results may differ from the reference program's by a relative error of at most 0.0058.
Values may be sent and summed in bfloat16 or wider, within the bound.
No kernel may reach another device: no remote copies, remote signals or barrier semaphores. Data moves between devices by JAX's collectives and lax.ppermute only.
A program may use at most 192 MiB of HBM per device.

```python
import math
import jax
import jax.numpy as jnp
import numpy as np
from jax import lax

HEADS = 16
KV_HEADS = 4
HEAD_DIM = 64
SEQ = 4096
QFEAT = 1024
KVFEAT = 256
GROUP = 4
N_KCOL = 8


def block_scale(stream_key, dims, pieces, smallest, top_value):
    def one(dim, parts):
        steps = jax.random.uniform(jax.random.fold_in(jax.random.fold_in(stream_key, 6), dim), (parts,), jnp.float32, smallest / len(pieces), top_value / len(pieces))
        return jnp.repeat(jnp.exp(steps), dims[dim] // parts).reshape((-1,) + (1,) * (len(dims) - dim - 1))

    loudness = one(*pieces[0])
    for cut in pieces[1:]:
        loudness = loudness * one(*cut)
    return loudness


def length_profile(number_of, total, most, slope):
    weights = [(1 << 20) // math.isqrt(standing ** slope) + 1 for standing in range(2, number_of + 1)]
    surplus, given = total - most - (number_of - 1), [1] * (number_of - 1)
    while surplus > 0:
        candidates = [i for i in range(number_of - 1) if given[i] < most]
        pool, budget = sum([weights[i] for i in candidates]), surplus
        for i in candidates:
            addition = min(most - given[i], max(1, budget * weights[i] // pool), surplus)
            given[i] = given[i] + addition
            surplus = surplus - addition
    return np.array([most] + given)


def ragged(rng, amount, total, limit, skew):
    if amount == 2:
        one = jax.random.randint(rng, (), max(1, total - limit), min(limit, total - 1) + 1)
        return jnp.stack([one, total - one])
    lengths = jnp.asarray(length_profile(amount, total, limit, skew), jnp.int32)
    couples = (amount - 1) // 2
    giver, receiver = lengths[1:1 + 2 * couples:2], lengths[2:2 + 2 * couples:2]
    margin = jnp.minimum(giver - 1, limit - receiver)
    passed = jax.random.randint(jax.random.fold_in(rng, 1), (couples,), 0, 1 << 20) % (margin + 1)
    lengths = lengths.at[1:1 + 2 * couples:2].set(giver - passed).at[2:2 + 2 * couples:2].set(receiver + passed)
    return lengths[jax.random.permutation(jax.random.fold_in(rng, 2), amount)]


def normal_values(stream_key, extent, spread, bound, shards=(), kind=jnp.bfloat16):
    factor_of = block_scale(stream_key, extent, shards, -0.22, 0.18) if shards else 1.0
    values = jax.random.normal(stream_key, extent, jnp.float32) * spread * factor_of
    return jnp.minimum(jnp.maximum(values, -bound), bound).astype(kind)


def setup_inputs(seed: int = 0) -> dict:
    seeds = jax.random.split(jax.random.key(seed), 8)
    return {
        "query": normal_values(seeds[0], (SEQ, QFEAT), 1.0, 6.0, ((0, 8), (1, 4))),
        "key": normal_values(seeds[1], (SEQ, KVFEAT), 1.0, 6.0, ((0, 32),)),
        "value": normal_values(seeds[2], (SEQ, KVFEAT), 1.0, 6.0, ((0, 32),)),
        "output": normal_values(seeds[3], (SEQ, QFEAT), 1.0, 6.0, ((0, 8), (1, 4))),
        "grad_out": normal_values(seeds[4], (SEQ, QFEAT), 1.0, 6.0, ((0, 8), (1, 4))),
        "lse": jnp.clip(2.0 + 3.0 * jax.random.uniform(seeds[5], (HEADS, SEQ), jnp.float32) ** block_scale(seeds[5], (HEADS, SEQ), ((0, 4), (1, 8)), -0.2, 0.2), 2.0, 5.0),
        "doc_ids": jnp.searchsorted(jnp.cumsum(ragged(seeds[6], max(8, SEQ // 1024), SEQ, SEQ // 2 + 2 * (SEQ // N_KCOL), 2)), jnp.arange(SEQ), side="right").astype(jnp.int32),
    }


score_scale = 0.125


def head_delta(grad_out, output):
    row_count = grad_out.shape[0]
    head_count = grad_out.shape[1] // HEAD_DIM
    product = grad_out.astype(jnp.float32) * output.astype(jnp.float32)
    return jnp.sum(product.reshape(row_count, head_count, HEAD_DIM), axis=2).T


def reference(query, key, value, output, grad_out, lse, doc_ids):
    delta = head_delta(grad_out, output)
    block_size = math.gcd(SEQ, 1024)
    block_count = SEQ // block_size
    positions = jnp.arange(SEQ, dtype=jnp.int32)

    def head_grads(head):
        kv_group = head // GROUP
        query_head = lax.dynamic_slice_in_dim(query, head * HEAD_DIM, HEAD_DIM, 1)
        grad_head = lax.dynamic_slice_in_dim(grad_out, head * HEAD_DIM, HEAD_DIM, 1)
        key_head = lax.dynamic_slice_in_dim(key, kv_group * HEAD_DIM, HEAD_DIM, 1)
        value_head = lax.dynamic_slice_in_dim(value, kv_group * HEAD_DIM, HEAD_DIM, 1)
        lse_row = lax.dynamic_index_in_dim(lse, head, 0, keepdims=False)
        delta_row = lax.dynamic_index_in_dim(delta, head, 0, keepdims=False)

        def block_step(totals, block_index):
            key_total, value_total = totals
            offset = block_index * block_size
            query_block = lax.dynamic_slice_in_dim(query_head, offset, block_size, 0)
            grad_block = lax.dynamic_slice_in_dim(grad_head, offset, block_size, 0)
            lse_block = lax.dynamic_slice_in_dim(lse_row, offset, block_size, 0)
            delta_block = lax.dynamic_slice_in_dim(delta_row, offset, block_size, 0)
            pos_block = lax.dynamic_slice_in_dim(positions, offset, block_size, 0)
            doc_block = lax.dynamic_slice_in_dim(doc_ids, offset, block_size, 0)
            scores = jnp.dot(query_block, key_head.T, preferred_element_type=jnp.float32) * score_scale
            live_mask = (positions[None, :] <= pos_block[:, None]) & (doc_ids[None, :] == doc_block[:, None])
            weights = jnp.where(live_mask, jnp.exp(scores - lse_block[:, None]), jnp.float32(0.0))
            value_total = value_total + jnp.dot(weights.astype(jnp.bfloat16).T, grad_block, preferred_element_type=jnp.float32)
            weight_grad = jnp.dot(grad_block, value_head.T, preferred_element_type=jnp.float32)
            score_grad = (weights * (weight_grad - delta_block[:, None])).astype(jnp.bfloat16)
            query_grad = jnp.dot(score_grad, key_head, preferred_element_type=jnp.float32) * score_scale
            key_total = key_total + jnp.dot(score_grad.T, query_block, preferred_element_type=jnp.float32) * score_scale
            return (key_total, value_total), query_grad

        zeros_init = jnp.zeros((SEQ, HEAD_DIM), jnp.float32)
        totals, query_grads = lax.scan(block_step, (zeros_init, zeros_init), jnp.arange(block_count, dtype=jnp.int32))
        return query_grads.reshape(SEQ, HEAD_DIM), totals[0], totals[1]

    query_all, key_all, value_all = lax.map(head_grads, jnp.arange(HEADS, dtype=jnp.int32))
    grad_query = jnp.transpose(query_all, (1, 0, 2)).reshape(SEQ, HEADS * HEAD_DIM)
    grad_key = jnp.transpose(key_all.reshape(KV_HEADS, GROUP, SEQ, HEAD_DIM).sum(axis=1), (1, 0, 2)).reshape(SEQ, KV_HEADS * HEAD_DIM)
    grad_value = jnp.transpose(value_all.reshape(KV_HEADS, GROUP, SEQ, HEAD_DIM).sum(axis=1), (1, 0, 2)).reshape(SEQ, KV_HEADS * HEAD_DIM)
    return (grad_query, grad_key, grad_value)
```

```python
import functools
import jax
import jax.numpy as jnp
from jax import lax
from jax.experimental import pallas as pl
from jax.experimental.pallas import tpu as pltpu
from jax.sharding import PartitionSpec as P

HEAD_DIM = 64
GROUP = 4
TILE = 512
LOG2E = 1.4426950408889634
SCORE_SCALE = 0.125

f32, bf16 = jnp.float32, jnp.bfloat16
VMEM_SPEC = pl.BlockSpec(memory_space=pltpu.VMEM)
SMEM_SPEC = pl.BlockSpec(memory_space=pltpu.SMEM)


def nt(a, b):
    return lax.dot_general(a, b, (((1,), (1,)), ((), ())), preferred_element_type=f32)


def nn(a, b):
    return lax.dot_general(a, b, (((1,), (0,)), ((), ())), preferred_element_type=f32)


def prep_kernel(panel, q0, q1, g0, g1, o0, o1, l0, l1, docs, q_all, g_all, q_t, g_t, stats):
    rows, feats = q0.shape
    heads = feats // HEAD_DIM
    tiles = rows // TILE
    col = lax.broadcasted_iota(jnp.int32, (feats, 128), 0) // HEAD_DIM
    lane = lax.broadcasted_iota(jnp.int32, (feats, 128), 1)
    pick = jnp.where(lane == col + heads, 1.0, 0.0).astype(bf16)
    for side, (q, g, o, l) in enumerate(((q0, g0, o0, l0), (q1, g1, o1, l1))):
        for t in range(tiles):
            at = slice(t * TILE, (t + 1) * TILE)
            dst = side * tiles + t
            qv, gv = q[at, :], g[at, :]
            q_all[dst] = qv
            g_all[dst] = gv
            q_t[dst] = (qv.astype(f32) * SCORE_SCALE).T.astype(bf16)
            g_t[dst] = gv.astype(f32).T.astype(bf16)
            product = gv.astype(f32) * o[at, :].astype(f32)
            high = product.astype(bf16)
            low = (product - high.astype(f32)).astype(bf16)
            delta = nn(high, pick) + nn(low, pick)
            doc_row = docs[pl.ds(panel[side] * tiles + t, 1), :]
            table = jnp.concatenate(
                [
                    l[:, at] * LOG2E,
                    jnp.zeros((heads, TILE), f32),
                    doc_row,
                    jnp.zeros((127 - 2 * heads, TILE), f32),
                ],
                axis=0,
            )
            stats[dst] = table.T + delta


def band_kernel(shift, heads, own, first_call, *refs):
    if first_call:
        panel, first, last, q_all, g_all, q_t, g_t, stats, docs, pair, dq, grads, acc = refs
    else:
        panel, first, last, q_all, g_all, q_t, g_t, stats, docs, pair, dq_in, dq, grads, acc = refs
    key_tiles = pair.shape[0] // TILE
    q_tiles = q_all.shape[0]
    if first_call:
        dq[...] = jnp.zeros_like(dq)
    acc[...] = jnp.zeros_like(acc)
    key_panel = panel[0] - shift

    def one(qt, kt, masked):
        keys = pl.ds(pl.multiple_of(kt * TILE, TILE), TILE)
        block = pair[keys, :]
        key = block[:, :HEAD_DIM]
        value = block[:, HEAD_DIM:]
        key_scaled = (key.astype(f32) * SCORE_SCALE).astype(bf16)
        side = qt // key_tiles
        q_base = (panel[side] * key_tiles + qt % key_tiles) * TILE
        k_base = (key_panel * key_tiles + kt) * TILE
        if masked:
            q_pos = lax.broadcasted_iota(jnp.int32, (TILE, TILE), 0) + (q_base - k_base)
            k_pos = lax.broadcasted_iota(jnp.int32, (TILE, TILE), 1)
            q_doc = stats[qt, :, 2 * heads : 2 * heads + 1]
            k_doc = docs[pl.ds(key_panel * key_tiles + kt, 1), :]
            live = (k_pos <= q_pos) & (q_doc == k_doc)
        parts = []
        key_sum = value_sum = None
        for h in range(heads):
            at = slice(h * HEAD_DIM, (h + 1) * HEAD_DIM)
            scores = nt(q_all[qt, :, at], key)
            weights = jnp.exp2(scores * (SCORE_SCALE * LOG2E) - stats[qt, :, h : h + 1])
            if masked:
                weights = jnp.where(live, weights, 0.0)
            weight_grad = nt(g_all[qt, :, at], value)
            score_grad = (weights * (weight_grad - stats[qt, :, heads + h : heads + h + 1])).astype(bf16)
            parts.append(nn(score_grad, key_scaled))
            value_part = nn(g_t[qt, at, :], weights.astype(bf16))
            key_part = nn(q_t[qt, at, :], score_grad)
            key_sum = key_part if key_sum is None else key_sum + key_part
            value_sum = value_part if value_sum is None else value_sum + value_part
        dq[qt] += jnp.concatenate(parts, axis=1)
        acc[:HEAD_DIM, keys] += key_sum
        acc[HEAD_DIM:, keys] += value_sum

    @pl.when(key_panel >= 0)
    def _():
        def step(index, carry):
            qt, kt = index // key_tiles, index % key_tiles
            side = qt // key_tiles
            q_at = panel[side] * key_tiles + qt % key_tiles
            k_at = key_panel * key_tiles + kt
            live = (k_at <= q_at) & (first[q_at] <= last[k_at])
            full = (k_at < q_at) & (first[k_at] == last[q_at])

            @pl.when(live & full)
            def _():
                one(qt, kt, False)

            @pl.when(live & jnp.logical_not(full))
            def _():
                one(qt, kt, True)

            return carry

        lax.fori_loop(0, q_tiles * key_tiles, step, 0)

    grads[...] = acc[...].astype(grads.dtype)
    if not first_call:
        del dq_in


def collect_kernel(own, *refs):
    parts, out = refs[:-1], refs[-1]
    total = own[...]
    for part in parts:
        total = total + part[...].astype(f32)
    chunk = out.shape[2]
    for i in range(out.shape[0]):
        out[i] = total[:, i * chunk : (i + 1) * chunk]


def finish_kernel(ways, got, grad_key, grad_value):
    heads = got.shape[0] // ways
    keys, values = [], []
    for g in range(heads):
        block = got[g * ways]
        for w in range(1, ways):
            block = block + got[g * ways + w]
        keys.append(block[:HEAD_DIM])
        values.append(block[HEAD_DIM:])
    grad_key[...] = jnp.concatenate(keys, axis=0).T
    grad_value[...] = jnp.concatenate(values, axis=0).T


def per_device(query, key, value, output, grad_out, lse, doc_ids):
    row_count, col_count = lax.axis_size("qrow"), lax.axis_size("kcol")
    col = lax.axis_index("kcol")
    rows, feats = query.shape
    heads = feats // HEAD_DIM
    key_rows, key_feats = key.shape
    pair_feats = 2 * HEAD_DIM
    tiles = rows // TILE
    q_tiles = 2 * tiles
    core_swap = [(i, i ^ 1) for i in range(col_count)]

    def swap(x):
        return lax.ppermute(x, "kcol", core_swap)

    q_other, g_other, o_other, l_other = swap(query), swap(grad_out), swap(output), swap(lse)

    pieces = []
    for r in range(row_count):
        g = r * heads // GROUP
        at = slice(g * HEAD_DIM, (g + 1) * HEAD_DIM)
        pieces.append(jnp.concatenate([key[:, at], value[:, at]], axis=1))
    pair = lax.all_to_all(jnp.stack(pieces), "qrow", 0, 0).reshape(rows, pair_feats)

    doc_tiles = doc_ids.reshape(-1, TILE)
    first, last = doc_tiles[:, 0], doc_tiles[:, TILE - 1]
    docs = doc_tiles.astype(f32)
    panel = jnp.stack([col, col ^ 1]).astype(jnp.int32)

    params = pltpu.CompilerParams(vmem_limit_bytes=48 << 20)
    q_all, g_all, q_t, g_t, stats = pl.pallas_call(
        prep_kernel,
        in_specs=[SMEM_SPEC] + [VMEM_SPEC] * 9,
        out_specs=[VMEM_SPEC] * 5,
        out_shape=[
            jax.ShapeDtypeStruct((q_tiles, TILE, feats), bf16),
            jax.ShapeDtypeStruct((q_tiles, TILE, feats), bf16),
            jax.ShapeDtypeStruct((q_tiles, feats, TILE), bf16),
            jax.ShapeDtypeStruct((q_tiles, feats, TILE), bf16),
            jax.ShapeDtypeStruct((q_tiles, TILE, 128), f32),
        ],
        compiler_params=params,
        name="prep",
    )(panel, query, q_other, grad_out, g_other, output, o_other, lse, l_other, docs)

    def band(distance, block, dq):
        own = distance == 0
        extra = [] if dq is None else [dq]
        return pl.pallas_call(
            functools.partial(band_kernel, 2 * distance, heads, own, dq is None),
            in_specs=[SMEM_SPEC] * 3 + [VMEM_SPEC] * (7 + len(extra)),
            out_specs=[VMEM_SPEC] * 2,
            out_shape=[
                jax.ShapeDtypeStruct((q_tiles, TILE, feats), f32),
                jax.ShapeDtypeStruct((pair_feats, rows), f32 if own else bf16),
            ],
            scratch_shapes=[pltpu.VMEM((pair_feats, rows), f32)],
            input_output_aliases={} if dq is None else {10: 0},
            compiler_params=params,
            cost_estimate=pl.CostEstimate(
                flops=10 * 2 * rows * rows * feats,
                bytes_accessed=6 << 20,
                transcendentals=2 * rows * rows * heads,
            ),
            name=f"band{distance}",
        )(panel, first, last, q_all, g_all, q_t, g_t, stats, docs, block, *extra)

    reach = min(col_count // 2 - 1, col_count // 4 + 1)
    blocks = {}
    for d in range(1, reach + 1):
        route = [(i, i + 2 * d) for i in range(col_count - 2 * d)]
        blocks[d] = lax.ppermute(pair, "kcol", route)
    dq = None
    returned = []
    for d in range(1, reach + 1):
        dq, grads = band(d, blocks[d], dq)
        route = [(i + 2 * d, i) for i in range(col_count - 2 * d)]
        returned.append(lax.ppermute(grads, "kcol", route))
    dq, own_grads = band(0, pair, dq)

    dq_partner = swap(dq[tiles:])
    grad_query = (dq[:tiles] + dq_partner).reshape(rows, feats)

    chunks = pl.pallas_call(
        collect_kernel,
        in_specs=[VMEM_SPEC] * (1 + reach),
        out_specs=VMEM_SPEC,
        out_shape=jax.ShapeDtypeStruct((row_count, pair_feats, key_rows), f32),
        name="collect",
    )(own_grads, *returned)
    got = lax.all_to_all(chunks, "qrow", 0, 0)
    grad_key, grad_value = pl.pallas_call(
        functools.partial(finish_kernel, row_count * HEAD_DIM // key_feats),
        in_specs=[VMEM_SPEC],
        out_specs=[VMEM_SPEC] * 2,
        out_shape=[jax.ShapeDtypeStruct((key_rows, key_feats), f32)] * 2,
        name="finish",
    )(got)
    return grad_query, grad_key, grad_value


def solution(mesh):
    return jax.shard_map(
        per_device,
        mesh=mesh,
        in_specs=(
            P("kcol", "qrow"),
            P(("kcol", "qrow"), None),
            P(("kcol", "qrow"), None),
            P("kcol", "qrow"),
            P("kcol", "qrow"),
            P("qrow", "kcol"),
            P(),
        ),
        out_specs=(P("kcol", "qrow"), P(("kcol", "qrow"), None), P(("kcol", "qrow"), None)),
        check_vma=False,
    )
```

```python
import functools
import jax
import jax.numpy as jnp
from jax import lax
from jax.experimental import pallas as pl
from jax.experimental.pallas import tpu as pltpu
from jax.sharding import PartitionSpec as P

HEAD_DIM = 64
GROUP = 4
DOCS = 16
FAR = 512.0
SUB = 256
LOG2E = 1.4426950408889634
SCORE_SCALE = 0.125

f32, bf16 = jnp.float32, jnp.bfloat16
VMEM_SPEC = pl.BlockSpec(memory_space=pltpu.VMEM)
SMEM_SPEC = pl.BlockSpec(memory_space=pltpu.SMEM)


def small(mib=4):
    return pltpu.CompilerParams(vmem_limit_bytes=mib << 20)


def nt(a, b):
    return lax.dot_general(a, b, (((1,), (1,)), ((), ())), preferred_element_type=f32)


def nn(a, b):
    return lax.dot_general(a, b, (((1,), (0,)), ((), ())), preferred_element_type=f32)


def halves_swapped(x):
    return jnp.concatenate([x[:, HEAD_DIM:], x[:, :HEAD_DIM]], axis=1)


def three(x):
    high = x.astype(bf16).astype(f32)
    rest = x - high
    middle = rest.astype(bf16).astype(f32)
    return high, middle, rest - middle


def one_hot_rows(doc_row, value):
    length = doc_row.shape[1]
    ids = lax.broadcasted_iota(jnp.int32, (DOCS, length), 0).astype(f32)
    return jnp.where(ids == doc_row, value, 0.0)


def pack_kernel(heads, key, value, out):
    for r in range(out.shape[0]):
        g = r * heads // GROUP
        at = slice(g * HEAD_DIM, (g + 1) * HEAD_DIM)
        out[r] = jnp.concatenate([key[:, at], value[:, at]], axis=1)


def prep_kernel(panel, q0, q1, g0, g1, o0, o1, l0, l1, docs, q_ext, g_ext, q_t, g_t):
    rows, feats = q0.shape
    heads = feats // HEAD_DIM
    lane = lax.broadcasted_iota(jnp.int32, (rows, 128), 1)
    low_half = lane < HEAD_DIM
    for side, (q, g, o, l) in enumerate(((q0, g0, o0, l0), (q1, g1, o1, l1))):
        dst = slice(side * rows, (side + 1) * rows)
        q_t[:, dst] = (q[...].astype(f32) * SCORE_SCALE).T.astype(bf16)
        g_t[:, dst] = g[...].astype(f32).T.astype(bf16)
        product = g[...].astype(f32) * o[...].astype(f32)
        high = product.astype(bf16)
        low = (product - high.astype(f32)).astype(bf16)
        doc_row = docs[pl.ds(panel[side], 1), :]
        tail = [one_hot_rows(doc_row, FAR), jnp.zeros((HEAD_DIM - 3 - DOCS, rows), f32)]
        for p in range(heads // 2):
            at = slice(p * 128, (p + 1) * 128)
            table = []
            for h in (2 * p + 1, 2 * p):
                table += list(three(-FAR - l[h : h + 1, :])) + tail
            extra = jnp.concatenate(table, axis=0).T
            q_pair = q[:, at].astype(f32) * SCORE_SCALE
            q_ext[2 * p, dst, :] = jnp.where(low_half, q_pair, extra).astype(bf16)
            q_ext[2 * p + 1, dst, :] = jnp.where(low_half, extra, q_pair).astype(bf16)
            col = lax.broadcasted_iota(jnp.int32, (feats, 128), 0) // HEAD_DIM
            spot = lax.broadcasted_iota(jnp.int32, (feats, 128), 1)
            even = (col == 2 * p) & (spot >= HEAD_DIM) & (spot < HEAD_DIM + 3)
            odd = (col == 2 * p + 1) & (spot < 3)
            pick = jnp.where(even | odd, -1.0, 0.0).astype(bf16)
            d0, d1, d2 = three(nn(high, pick) + nn(low, pick))
            place = lane % HEAD_DIM
            extra = jnp.where(place == 0, d0, jnp.where(place == 1, d1, d2))
            g_pair = g[:, at].astype(f32)
            g_ext[2 * p, dst, :] = jnp.where(low_half, g_pair, extra).astype(bf16)
            g_ext[2 * p + 1, dst, :] = jnp.where(low_half, extra, g_pair).astype(bf16)


def band_kernel(shift, q_tile, first_call, *refs):
    panel, first, last, q_ext, g_ext, q_t, g_t, docs, pair = refs[:9]
    dq, grads, acc, k_ext, v_ext, k_lone = refs[9 if first_call else 10 :]
    heads, q_rows, _ = q_ext.shape
    rows = pair.shape[0]
    subs = rows // SUB
    q_subs = q_tile // SUB
    q_tiles = q_rows // q_tile
    if first_call:
        dq[...] = jnp.zeros_like(dq)
    acc[...] = jnp.zeros_like(acc)
    key_panel = panel[0] - shift

    def one(qt, kt, masked):
        at_q = pl.ds(pl.multiple_of(qt * q_tile, q_tile), q_tile)
        at_k = pl.ds(pl.multiple_of(kt * SUB, SUB), SUB)
        weights, score_grads = [], []
        if masked:
            ahead = (qt % (rows // q_tile)) * q_tile - kt * SUB
            q_pos = lax.broadcasted_iota(jnp.int32, (q_tile, SUB), 0) + ahead
            live = lax.broadcasted_iota(jnp.int32, (q_tile, SUB), 1) <= q_pos
        for h in range(heads):
            weight = jnp.exp2(nt(q_ext[h, at_q, :], k_ext[h % 2, at_k, :]) * LOG2E)
            if masked:
                weight = jnp.where(live, weight, 0.0)
            grad = nt(g_ext[h, at_q, :], v_ext[h % 2, at_k, :])
            weights.append(weight.astype(bf16))
            score_grads.append((weight * grad).astype(bf16))
        key_sum = value_sum = 0.0
        for h in range(heads):
            at = slice(h * HEAD_DIM, (h + 1) * HEAD_DIM)
            key_sum += nn(q_t[at, at_q], score_grads[h])
            value_sum += nn(g_t[at, at_q], weights[h])
        for p in range(heads // 2):
            dq[at_q, p * 128 : (p + 1) * 128] += nn(score_grads[2 * p], k_lone[0, at_k, :]) + nn(
                score_grads[2 * p + 1], k_lone[1, at_k, :]
            )
        acc[:HEAD_DIM, at_k] += key_sum
        acc[HEAD_DIM:, at_k] += value_sum

    @pl.when(key_panel >= 0)
    def _():
        lane = lax.broadcasted_iota(jnp.int32, (rows, 128), 1)
        low_half = lane < HEAD_DIM
        doc_row = docs[pl.ds(key_panel, 1), :]
        half = [jnp.ones((3, rows), f32), one_hot_rows(doc_row, 1.0), jnp.zeros((HEAD_DIM - 3 - DOCS, rows), f32)]
        extra = jnp.concatenate(half + half, axis=0).T
        ones = jnp.where(lane % HEAD_DIM < 3, 1.0, 0.0)
        straight = pair[...].astype(f32)
        turned = halves_swapped(pair[...]).astype(f32)
        k_ext[0] = jnp.where(low_half, straight, extra).astype(bf16)
        k_ext[1] = jnp.where(low_half, extra, turned).astype(bf16)
        v_ext[0] = jnp.where(low_half, turned, ones).astype(bf16)
        v_ext[1] = jnp.where(low_half, ones, straight).astype(bf16)
        k_lone[0] = jnp.where(low_half, straight * SCORE_SCALE, 0.0).astype(bf16)
        k_lone[1] = jnp.where(low_half, 0.0, turned * SCORE_SCALE).astype(bf16)

        def step(index, carry):
            qt, kt = index // subs, index % subs
            side = qt // (rows // q_tile)
            q_at = panel[side] * subs + (qt % (rows // q_tile)) * q_subs
            k_at = key_panel * subs + kt
            live = first[q_at] <= last[k_at]
            if shift > 0:
                pl.when(live)(functools.partial(one, qt, kt, False))
            else:
                live = live & (k_at < q_at + q_subs)
                below = k_at < q_at
                pl.when(live & below)(functools.partial(one, qt, kt, False))
                pl.when(live & jnp.logical_not(below))(functools.partial(one, qt, kt, True))
            return carry

        lax.fori_loop(0, q_tiles * subs, step, 0)

    grads[...] = acc[...].astype(grads.dtype)


def collect_kernel(own, *refs):
    parts, out = refs[:-1], refs[-1]
    total = own[...]
    for part in parts:
        total = total + part[...].astype(f32)
    chunk = out.shape[2]
    for i in range(out.shape[0]):
        out[i] = total[:, i * chunk : (i + 1) * chunk]


def finish_kernel(ways, got, grad_key, grad_value):
    groups = got.shape[0] // ways
    keys, values = [], []
    for g in range(groups):
        block = got[g * ways]
        for w in range(1, ways):
            block = block + got[g * ways + w]
        keys.append(block[:HEAD_DIM])
        values.append(block[HEAD_DIM:])
    grad_key[...] = jnp.concatenate(keys, axis=0).T
    grad_value[...] = jnp.concatenate(values, axis=0).T


def per_device(query, key, value, output, grad_out, lse, doc_ids):
    row_count, col_count = lax.axis_size("qrow"), lax.axis_size("kcol")
    col = lax.axis_index("kcol")
    rows, feats = query.shape
    heads = feats // HEAD_DIM
    key_rows, key_feats = key.shape
    pair_feats = 2 * HEAD_DIM
    core_swap = [(i, i ^ 1) for i in range(col_count)]

    def swap(x):
        return lax.ppermute(x, "kcol", core_swap)

    q_other, g_other, o_other, l_other = swap(query), swap(grad_out), swap(output), swap(lse)

    pieces = pl.pallas_call(
        functools.partial(pack_kernel, heads),
        in_specs=[VMEM_SPEC] * 2,
        out_specs=VMEM_SPEC,
        out_shape=jax.ShapeDtypeStruct((row_count, key_rows, pair_feats), bf16),
        compiler_params=small(),
        name="pack",
    )(key, value)
    pair = lax.all_to_all(pieces, "qrow", 0, 0).reshape(rows, pair_feats)

    doc_subs = doc_ids.reshape(-1, SUB)
    first, last = doc_subs[:, 0], doc_subs[:, SUB - 1]
    docs = doc_ids.reshape(col_count, rows).astype(f32)
    panel = jnp.stack([col, col ^ 1]).astype(jnp.int32)

    q_ext, g_ext, q_t, g_t = pl.pallas_call(
        prep_kernel,
        in_specs=[SMEM_SPEC] + [VMEM_SPEC] * 9,
        out_specs=[VMEM_SPEC] * 4,
        out_shape=[jax.ShapeDtypeStruct((heads, 2 * rows, 128), bf16)] * 2
        + [jax.ShapeDtypeStruct((feats, 2 * rows), bf16)] * 2,
        compiler_params=small(16),
        name="prep",
    )(panel, query, q_other, grad_out, g_other, output, o_other, lse, l_other, docs)

    def band(distance, block, dq):
        own = distance == 0
        extra = [] if dq is None else [dq]
        return pl.pallas_call(
            functools.partial(band_kernel, 2 * distance, SUB if own else 2 * SUB, dq is None),
            in_specs=[SMEM_SPEC] * 3 + [VMEM_SPEC] * (6 + len(extra)),
            out_specs=[VMEM_SPEC] * 2,
            out_shape=[
                jax.ShapeDtypeStruct((2 * rows, feats), f32),
                jax.ShapeDtypeStruct((pair_feats, rows), f32 if own else bf16),
            ],
            scratch_shapes=[pltpu.VMEM((pair_feats, rows), f32)] + [pltpu.VMEM((2, rows, 128), bf16)] * 3,
            input_output_aliases={} if dq is None else {9: 0},
            compiler_params=small(24),
            cost_estimate=pl.CostEstimate(
                flops=20 * rows * rows * feats,
                bytes_accessed=6 << 20,
                transcendentals=2 * rows * rows * heads,
            ),
            name=f"band{distance}",
        )(panel, first, last, q_ext, g_ext, q_t, g_t, docs, block, *extra)

    reach = min(col_count // 2 - 1, col_count // 4 + 1)
    blocks = {}
    for d in range(1, reach + 1):
        route = [(i, i + 2 * d) for i in range(col_count - 2 * d)]
        blocks[d] = lax.ppermute(pair, "kcol", route)
    dq = None
    returned = []
    for d in range(1, reach + 1):
        dq, grads = band(d, blocks[d], dq)
        route = [(i + 2 * d, i) for i in range(col_count - 2 * d)]
        returned.append(lax.ppermute(grads, "kcol", route))
        if d > 1:
            dq, returned[-2] = lax.optimization_barrier((dq, returned[-2]))
    dq, own_grads = band(0, pair, dq)

    dq_partner = swap(dq[rows:])
    grad_query = dq[:rows] + dq_partner

    chunks = pl.pallas_call(
        collect_kernel,
        in_specs=[VMEM_SPEC] * (1 + reach),
        out_specs=VMEM_SPEC,
        out_shape=jax.ShapeDtypeStruct((row_count, pair_feats, key_rows), f32),
        compiler_params=small(),
        name="collect",
    )(own_grads, *returned)
    got = lax.all_to_all(chunks, "qrow", 0, 0)
    grad_key, grad_value = pl.pallas_call(
        functools.partial(finish_kernel, row_count * HEAD_DIM // key_feats),
        in_specs=[VMEM_SPEC],
        out_specs=[VMEM_SPEC] * 2,
        out_shape=[jax.ShapeDtypeStruct((key_rows, key_feats), f32)] * 2,
        compiler_params=small(),
        name="finish",
    )(got)
    return grad_query, grad_key, grad_value


def solution(mesh):
    return jax.shard_map(
        per_device,
        mesh=mesh,
        in_specs=(
            P("kcol", "qrow"),
            P(("kcol", "qrow"), None),
            P(("kcol", "qrow"), None),
            P("kcol", "qrow"),
            P("kcol", "qrow"),
            P("qrow", "kcol"),
            P(),
        ),
        out_specs=(P("kcol", "qrow"), P(("kcol", "qrow"), None), P(("kcol", "qrow"), None)),
        check_vma=False,
    )
```

```python
import functools
import jax
import jax.numpy as jnp
from jax import lax
from jax.experimental import pallas as pl
from jax.experimental.pallas import tpu as pltpu
from jax.sharding import PartitionSpec as P

HEAD_DIM = 64
GROUP = 4
DOCS = 16
FAR = 512.0
SUB = 256
EXTRA = 8
FAR_STEP = 2
PREP_MIB = 56
LOG2E = 1.4426950408889634
SCORE_SCALE = 0.125

f32, bf16 = jnp.float32, jnp.bfloat16
VMEM_SPEC = pl.BlockSpec(memory_space=pltpu.VMEM)
SMEM_SPEC = pl.BlockSpec(memory_space=pltpu.SMEM)


def small(mib=4):
    return pltpu.CompilerParams(vmem_limit_bytes=mib << 20)


def nt(a, b):
    return lax.dot_general(a, b, (((1,), (1,)), ((), ())), preferred_element_type=f32)


def nn(a, b):
    return lax.dot_general(a, b, (((1,), (0,)), ((), ())), preferred_element_type=f32)


def halves_swapped(x):
    return jnp.concatenate([x[:, HEAD_DIM:], x[:, :HEAD_DIM]], axis=1)


def three(x):
    high = x.astype(bf16).astype(f32)
    rest = x - high
    middle = rest.astype(bf16).astype(f32)
    return high, middle, rest - middle


def one_hot_rows(doc_row, value):
    length = doc_row.shape[1]
    ids = lax.broadcasted_iota(jnp.int32, (DOCS, length), 0).astype(f32)
    return jnp.where(ids == doc_row, value, 0.0)


def prep_kernel(key, value, query, grad_out, output, lse, pieces, packed):
    rows, feats = query.shape
    heads = feats // HEAD_DIM
    for r in range(pieces.shape[0]):
        g = r * heads // GROUP
        at = slice(g * HEAD_DIM, (g + 1) * HEAD_DIM)
        pieces[r] = jnp.concatenate([key[:, at], value[:, at]], axis=1)
    packed[:, :feats] = query[...]
    packed[:, feats : 2 * feats] = grad_out[...]
    product = grad_out[...].astype(f32) * output[...].astype(f32)
    high = product.astype(bf16)
    low = (product - high.astype(f32)).astype(bf16)
    head = lax.broadcasted_iota(jnp.int32, (feats, 128), 0) // HEAD_DIM
    spot = lax.broadcasted_iota(jnp.int32, (feats, 128), 1) - EXTRA * head
    pick = jnp.where((spot >= 3) & (spot < 6), -1.0, 0.0).astype(bf16)
    d0, d1, d2 = three(nn(high, pick) + nn(low, pick))
    table = []
    for h in range(heads):
        table += list(three(-FAR - lse[h : h + 1, :])) + [jnp.zeros((EXTRA - 3, rows), f32)]
    table.append(jnp.zeros((128 - EXTRA * heads, rows), f32))
    place = lax.broadcasted_iota(jnp.int32, (rows, 128), 1) % EXTRA
    delta = jnp.where(place == 3, d0, jnp.where(place == 4, d1, d2))
    packed[:, 2 * feats :] = (jnp.concatenate(table, axis=0).T + delta).astype(bf16)


def expand_kernel(sides, panel, *refs):
    packs, docs = refs[:sides], refs[sides]
    q_ext, g_ext, q_t, g_t = refs[sides + 1 :]
    feats = q_t.shape[0]
    heads = feats // HEAD_DIM
    rows = docs.shape[1]
    lane = lax.broadcasted_iota(jnp.int32, (rows, 128), 1)
    low_half = lane < HEAD_DIM
    source = lax.broadcasted_iota(jnp.int32, (128, 128), 0)
    target = lax.broadcasted_iota(jnp.int32, (128, 128), 1)
    offset = target % HEAD_DIM
    for side, packed in enumerate(packs):
        dst = slice(side * rows, (side + 1) * rows)
        doc_row = docs[pl.ds(panel[side], 1), :].astype(f32)
        half = [jnp.zeros((3, rows), f32), one_hot_rows(doc_row, FAR), jnp.zeros((HEAD_DIM - 3 - DOCS, rows), f32)]
        spread = jnp.concatenate(half + half, axis=0).T
        extra = packed[:, 2 * feats :]
        for p in range(heads // 2):
            at = slice(p * 128, (p + 1) * 128)
            q_pair = packed[:, at].astype(f32) * SCORE_SCALE
            g_pair = packed[:, feats + p * 128 : feats + (p + 1) * 128].astype(f32)
            q_t[at, dst] = q_pair.T.astype(bf16)
            g_t[at, dst] = g_pair.T.astype(bf16)
            base = EXTRA * jnp.where(target < HEAD_DIM, 2 * p + 1, 2 * p)
            move_q = jnp.where((source == base + offset) & (offset < 3), 1.0, 0.0).astype(bf16)
            move_g = jnp.where((source == base + 3 + offset) & (offset < 3), 1.0, 0.0).astype(bf16)
            q_more = nn(extra, move_q) + spread
            g_more = nn(extra, move_g)
            q_ext[2 * p, dst, :] = jnp.where(low_half, q_pair, q_more).astype(bf16)
            q_ext[2 * p + 1, dst, :] = jnp.where(low_half, q_more, q_pair).astype(bf16)
            g_ext[2 * p, dst, :] = jnp.where(low_half, g_pair, g_more).astype(bf16)
            g_ext[2 * p + 1, dst, :] = jnp.where(low_half, g_more, g_pair).astype(bf16)


def band_kernel(causal, q_tile, key_panels, chained, *refs):
    q_panel, k_panel, first, last, q_ext, g_ext, q_t, g_t, docs = refs[:9]
    pairs = refs[9 : 9 + key_panels]
    refs = refs[9 + key_panels + (1 if chained else 0) :]
    dq_out, grads = refs[0], refs[1 : 1 + key_panels]
    acc, k_ext, v_ext, k_lone, *more = refs[1 + key_panels :]
    dq = more[0] if more else dq_out
    heads, q_rows, _ = q_ext.shape
    rows = pairs[0].shape[0]
    subs = rows // SUB
    q_subs = q_tile // SUB
    per_panel = rows // q_tile
    q_tiles = q_rows // q_tile
    if not chained:
        dq[...] = jnp.zeros_like(dq)
    acc[...] = jnp.zeros_like(acc)

    def one(qt, kt, masked):
        at_q = pl.ds(pl.multiple_of(qt * q_tile, q_tile), q_tile)
        at_k = pl.ds(pl.multiple_of(kt * SUB, SUB), SUB)
        weights, score_grads = [], []
        if masked:
            ahead = (qt % per_panel) * q_tile - kt * SUB
            q_pos = lax.broadcasted_iota(jnp.int32, (q_tile, SUB), 0) + ahead
            live = lax.broadcasted_iota(jnp.int32, (q_tile, SUB), 1) <= q_pos
        for h in range(heads):
            weight = jnp.exp2(nt(q_ext[h, at_q, :], k_ext[h % 2, at_k, :]) * LOG2E)
            if masked:
                weight = jnp.where(live, weight, 0.0)
            grad = nt(g_ext[h, at_q, :], v_ext[h % 2, at_k, :])
            weights.append(weight.astype(bf16))
            score_grads.append((weight * grad).astype(bf16))
        key_sum = value_sum = 0.0
        for h in range(heads):
            at = slice(h * HEAD_DIM, (h + 1) * HEAD_DIM)
            key_sum += nn(q_t[at, at_q], score_grads[h])
            value_sum += nn(g_t[at, at_q], weights[h])
        for p in range(heads // 2):
            dq[at_q, p * 128 : (p + 1) * 128] += nn(score_grads[2 * p], k_lone[0, at_k, :]) + nn(
                score_grads[2 * p + 1], k_lone[1, at_k, :]
            )
        acc[:HEAD_DIM, at_k] += key_sum
        acc[HEAD_DIM:, at_k] += value_sum

    @pl.when((k_panel[0] >= 0) & (q_panel[0] >= 0))
    def _():
        lane = lax.broadcasted_iota(jnp.int32, (rows, 128), 1)
        low_half = lane < HEAD_DIM
        ones = jnp.where(lane % HEAD_DIM < 3, 1.0, 0.0)
        for j, pair in enumerate(pairs):
            dst = slice(j * rows, (j + 1) * rows)
            doc_row = docs[pl.ds(k_panel[j], 1), :].astype(f32)
            half = [
                jnp.ones((3, rows), f32),
                one_hot_rows(doc_row, 1.0),
                jnp.zeros((HEAD_DIM - 3 - DOCS, rows), f32),
            ]
            extra = jnp.concatenate(half + half, axis=0).T
            straight = pair[...].astype(f32)
            turned = halves_swapped(pair[...]).astype(f32)
            k_ext[0, dst, :] = jnp.where(low_half, straight, extra).astype(bf16)
            k_ext[1, dst, :] = jnp.where(low_half, extra, turned).astype(bf16)
            v_ext[0, dst, :] = jnp.where(low_half, turned, ones).astype(bf16)
            v_ext[1, dst, :] = jnp.where(low_half, ones, straight).astype(bf16)
            k_lone[0, dst, :] = jnp.where(low_half, straight * SCORE_SCALE, 0.0).astype(bf16)
            k_lone[1, dst, :] = jnp.where(low_half, 0.0, turned * SCORE_SCALE).astype(bf16)

        def step(index, carry):
            qt, kt = index // (subs * key_panels), index % (subs * key_panels)
            q_side, k_side = q_panel[qt // per_panel], k_panel[kt // subs]
            q_sub, k_sub = (qt % per_panel) * q_subs, kt % subs
            live = first[q_side * subs + q_sub] <= last[k_side * subs + k_sub]
            if not causal:
                pl.when(live)(functools.partial(one, qt, kt, False))
            else:
                q_at, k_at = q_side * subs + q_sub, k_side * subs + k_sub
                live = live & (k_at < q_at + q_subs)
                below = k_at < q_at
                pl.when(live & below)(functools.partial(one, qt, kt, False))
                pl.when(live & jnp.logical_not(below))(functools.partial(one, qt, kt, True))
            return carry

        lax.fori_loop(0, q_tiles * subs * key_panels, step, 0)

    for j in range(key_panels):
        grads[j][...] = acc[:, j * rows : (j + 1) * rows].astype(grads[j].dtype)
    if more:
        dq_out[...] = dq[...].astype(dq_out.dtype)


def collect_kernel(*refs):
    parts, out = refs[:-1], refs[-1]
    total = parts[0][...]
    for part in parts[1:]:
        total = total + part[...].astype(f32)
    chunk = out.shape[2]
    for i in range(out.shape[0]):
        out[i] = total[:, i * chunk : (i + 1) * chunk]


def finish_kernel(ways, count, got, dq, *refs):
    parts, (grad_query, grad_key, grad_value) = refs[:count], refs[count:]
    groups = got.shape[0] // ways
    keys, values = [], []
    for g in range(groups):
        block = got[g * ways]
        for w in range(1, ways):
            block = block + got[g * ways + w]
        keys.append(block[:HEAD_DIM])
        values.append(block[HEAD_DIM:])
    grad_key[...] = jnp.concatenate(keys, axis=0).T
    grad_value[...] = jnp.concatenate(values, axis=0).T
    total = dq[: grad_query.shape[0], :]
    for part in parts:
        total = total + part[...].astype(f32)
    grad_query[...] = total


def per_device(query, key, value, output, grad_out, lse, doc_ids):
    row_count, col_count = lax.axis_size("qrow"), lax.axis_size("kcol")
    col = lax.axis_index("kcol")
    rows, feats = query.shape
    heads = feats // HEAD_DIM
    key_rows, key_feats = key.shape
    pair_feats = 2 * HEAD_DIM
    chips = col_count // 2

    def swap(x):
        return lax.ppermute(x, "kcol", [(i, i ^ 1) for i in range(col_count)])

    def up(x, d):
        return lax.ppermute(x, "kcol", [(i, i + 2 * d) for i in range(col_count - 2 * d)])

    def down(x, d):
        return lax.ppermute(x, "kcol", [(i + 2 * d, i) for i in range(col_count - 2 * d)])

    pieces, packed = pl.pallas_call(
        prep_kernel,
        in_specs=[VMEM_SPEC] * 6,
        out_specs=[VMEM_SPEC] * 2,
        out_shape=[
            jax.ShapeDtypeStruct((row_count, key_rows, pair_feats), bf16),
            jax.ShapeDtypeStruct((rows, 2 * feats + 128), bf16),
        ],
        compiler_params=small(PREP_MIB),
        name="prep",
    )(key, value, query, grad_out, output, lse)
    pair = lax.all_to_all(pieces, "qrow", 0, 0).reshape(rows, pair_feats)
    packed_other = swap(packed)
    packed_far = down(packed, FAR_STEP)

    docs = doc_ids.reshape(col_count, rows)
    first, last = docs[:, ::SUB].reshape(-1), docs[:, SUB - 1 :: SUB].reshape(-1)

    def panels(*items):
        inside = [jnp.where((p >= 0) & (p < col_count), p, -1) for p in items]
        return jnp.stack(inside).astype(jnp.int32)

    mine = panels(col, col ^ 1)
    far = panels(col + 2 * FAR_STEP)

    def expand(panel, *packs):
        span = len(packs) * rows
        return pl.pallas_call(
            functools.partial(expand_kernel, len(packs)),
            in_specs=[SMEM_SPEC] + [VMEM_SPEC] * (len(packs) + 1),
            out_specs=[VMEM_SPEC] * 4,
            out_shape=[jax.ShapeDtypeStruct((heads, span, 128), bf16)] * 2
            + [jax.ShapeDtypeStruct((feats, span), bf16)] * 2,
            compiler_params=small(16),
            name=f"expand{len(packs)}",
        )(panel, *packs, docs)

    def band(name, q_panel, k_panel, queries, pairs, dq, q_tile, causal, out_types, dq_type=f32):
        chained = dq is not None
        extra = [dq] if chained else []
        count = len(pairs)
        q_rows = queries[0].shape[1]
        scratch = [pltpu.VMEM((pair_feats, count * rows), f32)] + [pltpu.VMEM((2, count * rows, 128), bf16)] * 3
        if dq_type != f32:
            scratch.append(pltpu.VMEM((q_rows, feats), f32))
        return pl.pallas_call(
            functools.partial(band_kernel, causal, q_tile, count, chained),
            in_specs=[SMEM_SPEC] * 4 + [VMEM_SPEC] * (5 + count + len(extra)),
            out_specs=[VMEM_SPEC] * (1 + count),
            out_shape=[jax.ShapeDtypeStruct((q_rows, feats), dq_type)]
            + [jax.ShapeDtypeStruct((pair_feats, rows), t) for t in out_types],
            scratch_shapes=scratch,
            input_output_aliases={9 + count: 0} if chained else {},
            compiler_params=small(24),
            cost_estimate=pl.CostEstimate(
                flops=10 * q_rows * count * rows * feats,
                bytes_accessed=6 << 20,
                transcendentals=q_rows * count * rows * heads,
            ),
            name=name,
        )(q_panel, k_panel, first, last, *queries, docs, *pairs, *extra)

    reach = min(chips - 1, chips // 2 + 1)
    steps = [d for d in range(1, reach + 1) if d != FAR_STEP]
    blocks = {d: up(pair, d) for d in steps}
    pair_other = swap(pair)

    queries = expand(mine, packed, packed_other)
    dq, own_grads = band("own", mine, panels(col), queries, [pair], None, SUB, True, [f32])
    grads = {}
    for d in steps:
        dq, grads[d] = band(
            f"band{d}", mine, panels(col - 2 * d), queries, [blocks[d]], dq, 2 * SUB, False, [bf16]
        )
    far_queries = expand(jnp.maximum(far, 0), packed_far)
    far_dq, far_own, far_other = band(
        "far", far, mine, far_queries, [pair, pair_other], None, 2 * SUB, False, [f32, bf16], bf16
    )
    dq, far_dq, far_other, *sent = lax.optimization_barrier((dq, far_dq, far_other, *[grads[d] for d in steps]))
    returned = [down(x, d) for x, d in zip(sent, steps)]
    returned.append(swap(far_other))
    dq_parts = [swap(dq[rows:]), up(far_dq, FAR_STEP)]

    chunks = pl.pallas_call(
        collect_kernel,
        in_specs=[VMEM_SPEC] * (2 + len(returned)),
        out_specs=VMEM_SPEC,
        out_shape=jax.ShapeDtypeStruct((row_count, pair_feats, key_rows), f32),
        compiler_params=small(),
        name="collect",
    )(own_grads, far_own, *returned)
    got = lax.all_to_all(chunks, "qrow", 0, 0)
    return pl.pallas_call(
        functools.partial(finish_kernel, row_count * HEAD_DIM // key_feats, len(dq_parts)),
        in_specs=[VMEM_SPEC] * (2 + len(dq_parts)),
        out_specs=[VMEM_SPEC] * 3,
        out_shape=[jax.ShapeDtypeStruct((rows, feats), f32)]
        + [jax.ShapeDtypeStruct((key_rows, key_feats), f32)] * 2,
        compiler_params=small(8),
        name="finish",
    )(got, dq, *dq_parts)


def solution(mesh):
    return jax.shard_map(
        per_device,
        mesh=mesh,
        in_specs=(
            P("kcol", "qrow"),
            P(("kcol", "qrow"), None),
            P(("kcol", "qrow"), None),
            P("kcol", "qrow"),
            P("kcol", "qrow"),
            P("qrow", "kcol"),
            P(),
        ),
        out_specs=(P("kcol", "qrow"), P(("kcol", "qrow"), None), P(("kcol", "qrow"), None)),
        check_vma=False,
    )
```

```python
import functools
import jax
import jax.numpy as jnp
from jax import lax
from jax.experimental import pallas as pl
from jax.experimental.pallas import tpu as pltpu
from jax.sharding import PartitionSpec as P

HEAD_DIM = 64
GROUP = 4
DOCS = 16
FAR = 512.0
SUB = 256
EXTRA = 8
LOG2E = 1.4426950408889634
SCORE_SCALE = 0.125

f32, bf16 = jnp.float32, jnp.bfloat16
VMEM_SPEC = pl.BlockSpec(memory_space=pltpu.VMEM)
SMEM_SPEC = pl.BlockSpec(memory_space=pltpu.SMEM)


def small(mib=4):
    return pltpu.CompilerParams(vmem_limit_bytes=mib << 20)


def nt(a, b):
    return lax.dot_general(a, b, (((1,), (1,)), ((), ())), preferred_element_type=f32)


def nn(a, b):
    return lax.dot_general(a, b, (((1,), (0,)), ((), ())), preferred_element_type=f32)


def halves_swapped(x):
    return jnp.concatenate([x[:, HEAD_DIM:], x[:, :HEAD_DIM]], axis=1)


def three(x):
    high = x.astype(bf16).astype(f32)
    rest = x - high
    middle = rest.astype(bf16).astype(f32)
    return high, middle, rest - middle


def one_hot_rows(doc_row, value):
    length = doc_row.shape[1]
    ids = lax.broadcasted_iota(jnp.int32, (DOCS, length), 0).astype(f32)
    return jnp.where(ids == doc_row, value, 0.0)


def prep_kernel(key, value, query, grad_out, output, lse, pieces, packed):
    rows, feats = query.shape
    heads = feats // HEAD_DIM
    for r in range(pieces.shape[0]):
        g = r * heads // GROUP
        at = slice(g * HEAD_DIM, (g + 1) * HEAD_DIM)
        pieces[r] = jnp.concatenate([key[:, at], value[:, at]], axis=1)
    packed[:, :feats] = query[...]
    packed[:, feats : 2 * feats] = grad_out[...]
    product = grad_out[...].astype(f32) * output[...].astype(f32)
    high = product.astype(bf16)
    low = (product - high.astype(f32)).astype(bf16)
    head = lax.broadcasted_iota(jnp.int32, (feats, 128), 0) // HEAD_DIM
    spot = lax.broadcasted_iota(jnp.int32, (feats, 128), 1) - EXTRA * head
    pick = jnp.where((spot >= 3) & (spot < 6), -1.0, 0.0).astype(bf16)
    d0, d1, d2 = three(nn(high, pick) + nn(low, pick))
    table = []
    for h in range(heads):
        table += list(three(-FAR - lse[h : h + 1, :])) + [jnp.zeros((EXTRA - 3, rows), f32)]
    table.append(jnp.zeros((128 - EXTRA * heads, rows), f32))
    place = lax.broadcasted_iota(jnp.int32, (rows, 128), 1) % EXTRA
    delta = jnp.where(place == 3, d0, jnp.where(place == 4, d1, d2))
    packed[:, 2 * feats :] = (jnp.concatenate(table, axis=0).T + delta).astype(bf16)


def expand_kernel(sides, panel, *refs):
    packs, docs = refs[:sides], refs[sides]
    q_ext, g_ext, q_t, g_t, docs_out = refs[sides + 1 :]
    docs_out[...] = docs[...]
    feats = q_t.shape[0]
    heads = feats // HEAD_DIM
    rows = docs.shape[1]
    lane = lax.broadcasted_iota(jnp.int32, (rows, 128), 1)
    low_half = lane < HEAD_DIM
    source = lax.broadcasted_iota(jnp.int32, (128, 128), 0)
    target = lax.broadcasted_iota(jnp.int32, (128, 128), 1)
    offset = target % HEAD_DIM
    for side, packed in enumerate(packs):
        dst = slice(side * rows, (side + 1) * rows)
        doc_row = docs[pl.ds(panel[side], 1), :].astype(f32)
        half = [jnp.zeros((3, rows), f32), one_hot_rows(doc_row, FAR), jnp.zeros((HEAD_DIM - 3 - DOCS, rows), f32)]
        spread = jnp.concatenate(half + half, axis=0).T
        extra = packed[:, 2 * feats :]
        for p in range(heads // 2):
            at = slice(p * 128, (p + 1) * 128)
            q_pair = packed[:, at].astype(f32) * SCORE_SCALE
            g_pair = packed[:, feats + p * 128 : feats + (p + 1) * 128].astype(f32)
            q_t[at, dst] = q_pair.T.astype(bf16)
            g_t[at, dst] = g_pair.T.astype(bf16)
            base = EXTRA * jnp.where(target < HEAD_DIM, 2 * p + 1, 2 * p)
            move_q = jnp.where((source == base + offset) & (offset < 3), 1.0, 0.0).astype(bf16)
            move_g = jnp.where((source == base + 3 + offset) & (offset < 3), 1.0, 0.0).astype(bf16)
            q_more = nn(extra, move_q) + spread
            g_more = nn(extra, move_g)
            q_ext[2 * p, dst, :] = jnp.where(low_half, q_pair, q_more).astype(bf16)
            q_ext[2 * p + 1, dst, :] = jnp.where(low_half, q_more, q_pair).astype(bf16)
            g_ext[2 * p, dst, :] = jnp.where(low_half, g_pair, g_more).astype(bf16)
            g_ext[2 * p + 1, dst, :] = jnp.where(low_half, g_more, g_pair).astype(bf16)


def band_kernel(causal, q_tile, chained, returns, q_base, *refs):
    q_panel, k_panel, first, last, q_ext, g_ext, q_t, g_t, docs, pair = refs[:10]
    refs = refs[10 + (1 if chained else 0) :]
    parts, refs = refs[:returns], refs[returns:]
    dq, out, acc, k_ext, v_ext, k_lone = refs
    heads, q_rows, _ = q_ext.shape
    rows = pair.shape[0]
    subs = rows // SUB
    q_subs = q_tile // SUB
    per_panel = rows // q_tile
    q_tiles = q_panel.shape[0] * per_panel
    if not chained:
        dq[...] = jnp.zeros_like(dq)
    if returns:
        total = parts[0][...].astype(f32)
        for part in parts[1:]:
            total = total + part[...].astype(f32)
        acc[...] = total
    else:
        acc[...] = jnp.zeros_like(acc)

    def one(qt, kt, masked):
        at_q = pl.ds(pl.multiple_of(q_base * rows + qt * q_tile, q_tile), q_tile)
        at_k = pl.ds(pl.multiple_of(kt * SUB, SUB), SUB)
        weights, score_grads = [], []
        if masked:
            ahead = (qt % per_panel) * q_tile - kt * SUB
            q_pos = lax.broadcasted_iota(jnp.int32, (q_tile, SUB), 0) + ahead
            live = lax.broadcasted_iota(jnp.int32, (q_tile, SUB), 1) <= q_pos
        for h in range(heads):
            weight = jnp.exp2(nt(q_ext[h, at_q, :], k_ext[h % 2, at_k, :]) * LOG2E)
            if masked:
                weight = jnp.where(live, weight, 0.0)
            grad = nt(g_ext[h, at_q, :], v_ext[h % 2, at_k, :])
            weights.append(weight.astype(bf16))
            score_grads.append((weight * grad).astype(bf16))
        key_sum = value_sum = 0.0
        for h in range(heads):
            at = slice(h * HEAD_DIM, (h + 1) * HEAD_DIM)
            key_sum += nn(q_t[at, at_q], score_grads[h])
            value_sum += nn(g_t[at, at_q], weights[h])
        for p in range(heads // 2):
            dq[at_q, p * 128 : (p + 1) * 128] += nn(score_grads[2 * p], k_lone[0, at_k, :]) + nn(
                score_grads[2 * p + 1], k_lone[1, at_k, :]
            )
        acc[:HEAD_DIM, at_k] += key_sum
        acc[HEAD_DIM:, at_k] += value_sum

    key_side = k_panel[0]
    some = first[q_panel[0] * subs] <= last[jnp.maximum(key_side, 0) * subs + subs - 1]
    for j in range(1, q_panel.shape[0]):
        some = some | (first[q_panel[j] * subs] <= last[jnp.maximum(key_side, 0) * subs + subs - 1])
    some = some & (key_side >= 0)
    if causal:
        reach = key_side <= q_panel[0]
        for j in range(1, q_panel.shape[0]):
            reach = reach | (key_side <= q_panel[j])
        some = some & reach

    @pl.when(some)
    def _():
        lane = lax.broadcasted_iota(jnp.int32, (rows, 128), 1)
        low_half = lane < HEAD_DIM
        ones = jnp.where(lane % HEAD_DIM < 3, 1.0, 0.0)
        doc_row = docs[pl.ds(key_side, 1), :].astype(f32)
        half = [jnp.ones((3, rows), f32), one_hot_rows(doc_row, 1.0), jnp.zeros((HEAD_DIM - 3 - DOCS, rows), f32)]
        extra = jnp.concatenate(half + half, axis=0).T
        straight = pair[...].astype(f32)
        turned = halves_swapped(pair[...]).astype(f32)
        k_ext[0] = jnp.where(low_half, straight, extra).astype(bf16)
        k_ext[1] = jnp.where(low_half, extra, turned).astype(bf16)
        v_ext[0] = jnp.where(low_half, turned, ones).astype(bf16)
        v_ext[1] = jnp.where(low_half, ones, straight).astype(bf16)
        k_lone[0] = jnp.where(low_half, straight * SCORE_SCALE, 0.0).astype(bf16)
        k_lone[1] = jnp.where(low_half, 0.0, turned * SCORE_SCALE).astype(bf16)

        def step(index, carry):
            qt, kt = index // subs, index % subs
            q_at = q_panel[qt // per_panel] * subs + (qt % per_panel) * q_subs
            k_at = key_side * subs + kt
            live = first[q_at] <= last[k_at]
            if not causal:
                pl.when(live)(functools.partial(one, qt, kt, False))
            else:
                live = live & (k_at < q_at + q_subs)
                below = k_at < q_at
                pl.when(live & below)(functools.partial(one, qt, kt, False))
                pl.when(live & jnp.logical_not(below))(functools.partial(one, qt, kt, True))
            return carry

        lax.fori_loop(0, q_tiles * subs, step, 0)

    if len(out.shape) == 3:
        chunk = out.shape[2]
        for i in range(out.shape[0]):
            out[i] = acc[:, i * chunk : (i + 1) * chunk]
    else:
        out[...] = acc[...].astype(out.dtype)


def finish_kernel(ways, count, got, dq, *refs):
    parts, (grad_query, grad_key, grad_value) = refs[:count], refs[count:]
    groups = got.shape[0] // ways
    keys, values = [], []
    for g in range(groups):
        block = got[g * ways]
        for w in range(1, ways):
            block = block + got[g * ways + w]
        keys.append(block[:HEAD_DIM])
        values.append(block[HEAD_DIM:])
    grad_key[...] = jnp.concatenate(keys, axis=0).T
    grad_value[...] = jnp.concatenate(values, axis=0).T
    total = dq[: grad_query.shape[0], :]
    for part in parts:
        total = total + part[...].astype(f32)
    grad_query[...] = total


def per_device(query, key, value, output, grad_out, lse, doc_ids):
    row_count, col_count = lax.axis_size("qrow"), lax.axis_size("kcol")
    col = lax.axis_index("kcol")
    rows, feats = query.shape
    heads = feats // HEAD_DIM
    key_rows, key_feats = key.shape
    pair_feats = 2 * HEAD_DIM
    chips = col_count // 2

    def swap(x):
        return lax.ppermute(x, "kcol", [(i, i ^ 1) for i in range(col_count)])

    def up(x, d):
        return lax.ppermute(x, "kcol", [(i, i + 2 * d) for i in range(col_count - 2 * d)])

    def down(x, d):
        return lax.ppermute(x, "kcol", [(i + 2 * d, i) for i in range(col_count - 2 * d)])

    pieces, packed = pl.pallas_call(
        prep_kernel,
        in_specs=[VMEM_SPEC] * 6,
        out_specs=[VMEM_SPEC] * 2,
        out_shape=[
            jax.ShapeDtypeStruct((row_count, key_rows, pair_feats), bf16),
            jax.ShapeDtypeStruct((rows, 2 * feats + 128), bf16),
        ],
        compiler_params=small(56),
        name="prep",
    )(key, value, query, grad_out, output, lse)
    packed_other = swap(packed)
    pair = lax.all_to_all(pieces, "qrow", 0, 0).reshape(rows, pair_feats)

    docs = doc_ids.reshape(col_count, rows)
    first, last = docs[:, ::SUB].reshape(-1), docs[:, SUB - 1 :: SUB].reshape(-1)
    mine = jnp.stack([col, col ^ 1]).astype(jnp.int32)

    q_ext, g_ext, q_t, g_t, docs = pl.pallas_call(
        functools.partial(expand_kernel, 2),
        in_specs=[SMEM_SPEC] + [VMEM_SPEC] * 3,
        out_specs=[VMEM_SPEC] * 5,
        out_shape=[jax.ShapeDtypeStruct((heads, 2 * rows, 128), bf16)] * 2
        + [jax.ShapeDtypeStruct((feats, 2 * rows), bf16)] * 2
        + [jax.ShapeDtypeStruct(docs.shape, jnp.int32)],
        compiler_params=small(16),
        name="expand",
    )(mine, packed, packed_other, docs)
    pair, docs = lax.optimization_barrier((pair, docs))

    def band(name, q_panel, k_panel, block, dq, parts, q_tile, causal, q_base, out):
        chained = dq is not None
        extra = [dq] if chained else []
        return pl.pallas_call(
            functools.partial(band_kernel, causal, q_tile, chained, len(parts), q_base),
            in_specs=[SMEM_SPEC] * 4 + [VMEM_SPEC] * (6 + len(extra) + len(parts)),
            out_specs=[VMEM_SPEC] * 2,
            out_shape=[jax.ShapeDtypeStruct((2 * rows, feats), f32), out],
            scratch_shapes=[pltpu.VMEM((pair_feats, rows), f32)] + [pltpu.VMEM((2, rows, 128), bf16)] * 3,
            input_output_aliases={10: 0} if chained else {},
            compiler_params=small(24),
            cost_estimate=pl.CostEstimate(
                flops=20 * rows * rows * feats,
                bytes_accessed=6 << 20,
                transcendentals=2 * rows * rows * heads,
            ),
            name=name,
        )(q_panel, k_panel, first, last, q_ext, g_ext, q_t, g_t, docs, block, *extra, *parts)

    reach = min(chips - 1, chips // 2 + 1)
    order = [*range(2, reach + 1), 1]
    blocks = {d: up(pair, d) for d in order}
    wire = jax.ShapeDtypeStruct((pair_feats, rows), bf16)
    dq = None
    back = []
    for d in order:
        panel = (col - 2 * d).astype(jnp.int32)[None]
        dq, grads = band(f"band{d}", mine, panel, blocks[d], dq, [], 2 * SUB if d < reach else SUB, False, 0, wire)
        back.append(down(grads, d))
    dq, *early = lax.optimization_barrier((dq, *back[:-1]))
    here = mine[:1]
    dq, own = band(
        "own1", mine[1:], here, pair, dq, [], 2 * SUB, True, 1, jax.ShapeDtypeStruct((pair_feats, rows), f32)
    )
    dq, chunks = band(
        "own0", here, here, pair, dq, [own, *early, back[-1]], SUB, True, 0,
        jax.ShapeDtypeStruct((row_count, pair_feats, key_rows), f32),
    )
    dq_parts = [swap(dq[rows:])]
    got = lax.all_to_all(chunks, "qrow", 0, 0)
    return pl.pallas_call(
        functools.partial(finish_kernel, row_count * HEAD_DIM // key_feats, len(dq_parts)),
        in_specs=[VMEM_SPEC] * (2 + len(dq_parts)),
        out_specs=[VMEM_SPEC] * 3,
        out_shape=[jax.ShapeDtypeStruct((rows, feats), f32)]
        + [jax.ShapeDtypeStruct((key_rows, key_feats), f32)] * 2,
        compiler_params=small(8),
        name="finish",
    )(got, dq, *dq_parts)


def solution(mesh):
    return jax.shard_map(
        per_device,
        mesh=mesh,
        in_specs=(
            P("kcol", "qrow"),
            P(("kcol", "qrow"), None),
            P(("kcol", "qrow"), None),
            P("kcol", "qrow"),
            P("kcol", "qrow"),
            P("qrow", "kcol"),
            P(),
        ),
        out_specs=(P("kcol", "qrow"), P(("kcol", "qrow"), None), P(("kcol", "qrow"), None)),
        check_vma=False,
    )
```

```python
import functools
import jax
import jax.numpy as jnp
from jax import lax
from jax.experimental import pallas as pl
from jax.experimental.pallas import tpu as pltpu
from jax.sharding import PartitionSpec as P

HEAD_DIM = 64
GROUP = 4
DOCS = 16
FAR = 512.0
SUB = 256
EXTRA = 8
LOG2E = 1.4426950408889634
SCORE_SCALE = 0.125

f32, bf16 = jnp.float32, jnp.bfloat16
VMEM_SPEC = pl.BlockSpec(memory_space=pltpu.VMEM)
SMEM_SPEC = pl.BlockSpec(memory_space=pltpu.SMEM)


def small(mib=4):
    return pltpu.CompilerParams(vmem_limit_bytes=mib << 20)


def nt(a, b):
    return lax.dot_general(a, b, (((1,), (1,)), ((), ())), preferred_element_type=f32)


def nn(a, b):
    return lax.dot_general(a, b, (((1,), (0,)), ((), ())), preferred_element_type=f32)


def halves_swapped(x):
    return jnp.concatenate([x[:, HEAD_DIM:], x[:, :HEAD_DIM]], axis=1)


def three(x):
    high = x.astype(bf16).astype(f32)
    rest = x - high
    middle = rest.astype(bf16).astype(f32)
    return high, middle, rest - middle


def one_hot_rows(doc_row, value):
    length = doc_row.shape[1]
    ids = lax.broadcasted_iota(jnp.int32, (DOCS, length), 0).astype(f32)
    return jnp.where(ids == doc_row, value, 0.0)


def prep_kernel(place, key, value, query, grad_out, output, lse, *refs):
    pieces, packed, stage = refs[:-2], refs[-2], refs[-1]
    rows, feats = query.shape
    heads = feats // HEAD_DIM
    for r in range(len(pieces)):
        g = r * heads // GROUP
        at = slice(g * HEAD_DIM, (g + 1) * HEAD_DIM)
        stage[r] = jnp.concatenate([key[:, at], value[:, at]], axis=1)
    for j, piece in enumerate(pieces):
        piece[...] = stage[place[0] ^ j]
    packed[:, :feats] = query[...]
    packed[:, feats : 2 * feats] = grad_out[...]
    product = grad_out[...].astype(f32) * output[...].astype(f32)
    high = product.astype(bf16)
    low = (product - high.astype(f32)).astype(bf16)
    head = lax.broadcasted_iota(jnp.int32, (feats, 128), 0) // HEAD_DIM
    spot = lax.broadcasted_iota(jnp.int32, (feats, 128), 1) - EXTRA * head
    pick = jnp.where((spot >= 3) & (spot < 6), -1.0, 0.0).astype(bf16)
    d0, d1, d2 = three(nn(high, pick) + nn(low, pick))
    table = []
    for h in range(heads):
        table += list(three(-FAR - lse[h : h + 1, :])) + [jnp.zeros((EXTRA - 3, rows), f32)]
    table.append(jnp.zeros((128 - EXTRA * heads, rows), f32))
    place = lax.broadcasted_iota(jnp.int32, (rows, 128), 1) % EXTRA
    delta = jnp.where(place == 3, d0, jnp.where(place == 4, d1, d2))
    packed[:, 2 * feats :] = (jnp.concatenate(table, axis=0).T + delta).astype(bf16)


def join_kernel(place, *refs):
    parts, out = refs[:-1], refs[-1]
    length = parts[0].shape[0]
    for j, part in enumerate(parts):
        out[pl.ds(pl.multiple_of((place[0] ^ j) * length, length), length), :] = part[...]


def expand_kernel(sides, panel, first, last, *refs):
    packs, docs = refs[:sides], refs[sides]
    q_ext, g_ext, q_t, g_t, docs_out = refs[sides + 1 :]
    docs_out[...] = docs[...]
    feats = q_t.shape[0]
    heads = feats // HEAD_DIM
    rows = docs.shape[1]
    lane = lax.broadcasted_iota(jnp.int32, (rows, 128), 1)
    low_half = lane < HEAD_DIM
    source = lax.broadcasted_iota(jnp.int32, (128, 128), 0)
    target = lax.broadcasted_iota(jnp.int32, (128, 128), 1)
    offset = target % HEAD_DIM
    for side, packed in enumerate(packs):
        dst = slice(side * rows, (side + 1) * rows)
        doc_row = docs[pl.ds(panel[side], 1), :].astype(f32)
        half = [jnp.zeros((3, rows), f32), one_hot_rows(doc_row, FAR), jnp.zeros((HEAD_DIM - 3 - DOCS, rows), f32)]
        spread = jnp.concatenate(half + half, axis=0).T
        extra = packed[:, 2 * feats :]
        for p in range(heads // 2):
            at = slice(p * 128, (p + 1) * 128)
            q_pair = packed[:, at].astype(f32) * SCORE_SCALE
            g_pair = packed[:, feats + p * 128 : feats + (p + 1) * 128].astype(f32)
            q_t[at, dst] = q_pair.T.astype(bf16)
            g_t[at, dst] = g_pair.T.astype(bf16)
            base = EXTRA * jnp.where(target < HEAD_DIM, 2 * p + 1, 2 * p)
            move_q = jnp.where((source == base + offset) & (offset < 3), 1.0, 0.0).astype(bf16)
            move_g = jnp.where((source == base + 3 + offset) & (offset < 3), 1.0, 0.0).astype(bf16)
            q_more = nn(extra, move_q) + spread
            g_more = nn(extra, move_g)
            q_ext[2 * p, dst, :] = jnp.where(low_half, q_pair, q_more).astype(bf16)
            q_ext[2 * p + 1, dst, :] = jnp.where(low_half, q_more, q_pair).astype(bf16)
            g_ext[2 * p, dst, :] = jnp.where(low_half, g_pair, g_more).astype(bf16)
            g_ext[2 * p + 1, dst, :] = jnp.where(low_half, g_more, g_pair).astype(bf16)


def band_kernel(causal, q_tile, chained, returns, q_base, *refs):
    place, q_panel, k_panel, first, last, q_ext, g_ext, q_t, g_t, docs, pair = refs[:11]
    refs = refs[11 + (1 if chained else 0) :]
    parts, refs = refs[:returns], refs[returns:]
    dq, *outs, acc, k_ext, v_ext, k_lone = refs
    heads, q_rows, _ = q_ext.shape
    rows = pair.shape[0]
    subs = rows // SUB
    q_subs = q_tile // SUB
    per_panel = rows // q_tile
    q_tiles = q_panel.shape[0] * per_panel
    if not chained:
        dq[...] = jnp.zeros_like(dq)
    if returns:
        total = parts[0][...].astype(f32)
        for part in parts[1:]:
            total = total + part[...].astype(f32)
        acc[...] = total
    else:
        acc[...] = jnp.zeros_like(acc)

    def one(qt, kt, masked):
        at_q = pl.ds(pl.multiple_of(q_base * rows + qt * q_tile, q_tile), q_tile)
        at_k = pl.ds(pl.multiple_of(kt * SUB, SUB), SUB)
        weights, score_grads = [], []
        if masked:
            ahead = (qt % per_panel) * q_tile - kt * SUB
            q_pos = lax.broadcasted_iota(jnp.int32, (q_tile, SUB), 0) + ahead
            live = lax.broadcasted_iota(jnp.int32, (q_tile, SUB), 1) <= q_pos
        for h in range(heads):
            weight = jnp.exp2(nt(q_ext[h, at_q, :], k_ext[h % 2, at_k, :]) * LOG2E)
            if masked:
                weight = jnp.where(live, weight, 0.0)
            grad = nt(g_ext[h, at_q, :], v_ext[h % 2, at_k, :])
            weights.append(weight.astype(bf16))
            score_grads.append((weight * grad).astype(bf16))
        key_sum = value_sum = 0.0
        for h in range(heads):
            at = slice(h * HEAD_DIM, (h + 1) * HEAD_DIM)
            key_sum += nn(q_t[at, at_q], score_grads[h])
            value_sum += nn(g_t[at, at_q], weights[h])
        for p in range(heads // 2):
            dq[at_q, p * 128 : (p + 1) * 128] += nn(score_grads[2 * p], k_lone[0, at_k, :]) + nn(
                score_grads[2 * p + 1], k_lone[1, at_k, :]
            )
        acc[:HEAD_DIM, at_k] += key_sum
        acc[HEAD_DIM:, at_k] += value_sum

    key_side = k_panel[0]
    some = first[q_panel[0] * subs] <= last[jnp.maximum(key_side, 0) * subs + subs - 1]
    for j in range(1, q_panel.shape[0]):
        some = some | (first[q_panel[j] * subs] <= last[jnp.maximum(key_side, 0) * subs + subs - 1])
    some = some & (key_side >= 0)
    if causal:
        reach = key_side <= q_panel[0]
        for j in range(1, q_panel.shape[0]):
            reach = reach | (key_side <= q_panel[j])
        some = some & reach

    @pl.when(some)
    def _():
        lane = lax.broadcasted_iota(jnp.int32, (rows, 128), 1)
        low_half = lane < HEAD_DIM
        ones = jnp.where(lane % HEAD_DIM < 3, 1.0, 0.0)
        doc_row = docs[pl.ds(key_side, 1), :].astype(f32)
        half = [jnp.ones((3, rows), f32), one_hot_rows(doc_row, 1.0), jnp.zeros((HEAD_DIM - 3 - DOCS, rows), f32)]
        extra = jnp.concatenate(half + half, axis=0).T
        straight = pair[...].astype(f32)
        turned = halves_swapped(pair[...]).astype(f32)
        k_ext[0] = jnp.where(low_half, straight, extra).astype(bf16)
        k_ext[1] = jnp.where(low_half, extra, turned).astype(bf16)
        v_ext[0] = jnp.where(low_half, turned, ones).astype(bf16)
        v_ext[1] = jnp.where(low_half, ones, straight).astype(bf16)
        k_lone[0] = jnp.where(low_half, straight * SCORE_SCALE, 0.0).astype(bf16)
        k_lone[1] = jnp.where(low_half, 0.0, turned * SCORE_SCALE).astype(bf16)

        def step(index, carry):
            qt, kt = index // subs, index % subs
            q_at = q_panel[qt // per_panel] * subs + (qt % per_panel) * q_subs
            k_at = key_side * subs + kt
            live = first[q_at] <= last[k_at]
            if not causal:
                pl.when(live)(functools.partial(one, qt, kt, False))
            else:
                live = live & (k_at < q_at + q_subs)
                below = k_at < q_at
                pl.when(live & below)(functools.partial(one, qt, kt, False))
                pl.when(live & jnp.logical_not(below))(functools.partial(one, qt, kt, True))
            return carry

        lax.fori_loop(0, q_tiles * subs, step, 0)

    if len(outs) > 1:
        chunk = outs[0].shape[1]
        for j, out in enumerate(outs):
            out[...] = acc[:, pl.ds(pl.multiple_of((place[0] ^ j) * chunk, chunk), chunk)]
    else:
        outs[0][...] = acc[...].astype(outs[0].dtype)


def finish_kernel(ways, count, place, dq, *refs):
    chunks, (other,), (grad_query, grad_key, grad_value, got) = refs[:count], refs[count : count + 1], refs[count + 1 :]
    for j, chunk in enumerate(chunks):
        got[place[0] ^ j] = chunk[...]
    keys, values = [], []
    for g in range(count // ways):
        block = got[g * ways]
        for w in range(1, ways):
            block = block + got[g * ways + w]
        keys.append(block[:HEAD_DIM])
        values.append(block[HEAD_DIM:])
    grad_key[...] = jnp.concatenate(keys, axis=0).T
    grad_value[...] = jnp.concatenate(values, axis=0).T
    grad_query[...] = dq[: grad_query.shape[0], :] + other[...]


def per_device(query, key, value, output, grad_out, lse, doc_ids):
    row_count, col_count = lax.axis_size("qrow"), lax.axis_size("kcol")
    col = lax.axis_index("kcol")
    rows, feats = query.shape
    heads = feats // HEAD_DIM
    key_rows, key_feats = key.shape
    pair_feats = 2 * HEAD_DIM
    chips = col_count // 2

    def swap(x):
        return lax.ppermute(x, "kcol", [(i, i ^ 1) for i in range(col_count)])

    def up(x, d):
        return lax.ppermute(x, "kcol", [(i, i + 2 * d) for i in range(col_count - 2 * d)])

    def down(x, d):
        return lax.ppermute(x, "kcol", [(i + 2 * d, i) for i in range(col_count - 2 * d)])

    def across(x, j):
        return lax.ppermute(x, "qrow", [(i, i ^ j) for i in range(row_count)]) if j else x

    place = lax.axis_index("qrow").astype(jnp.int32)[None]
    *pieces, packed = pl.pallas_call(
        prep_kernel,
        in_specs=[SMEM_SPEC] + [VMEM_SPEC] * 6,
        out_specs=[VMEM_SPEC] * (row_count + 1),
        out_shape=[jax.ShapeDtypeStruct((key_rows, pair_feats), bf16)] * row_count
        + [jax.ShapeDtypeStruct((rows, 2 * feats + 128), bf16)],
        scratch_shapes=[pltpu.VMEM((row_count, key_rows, pair_feats), bf16)],
        compiler_params=small(56),
        name="prep",
    )(place, key, value, query, grad_out, output, lse)
    packed_other = swap(packed)
    pieces = [across(x, j) for j, x in enumerate(pieces)]

    docs = doc_ids.reshape(col_count, rows)
    first, last = docs[:, ::SUB].reshape(-1), docs[:, SUB - 1 :: SUB].reshape(-1)
    mine = jnp.stack([col, col ^ 1]).astype(jnp.int32)

    q_ext, g_ext, q_t, g_t, docs = pl.pallas_call(
        functools.partial(expand_kernel, 2),
        in_specs=[SMEM_SPEC] * 3 + [VMEM_SPEC] * 3,
        out_specs=[VMEM_SPEC] * 5,
        out_shape=[jax.ShapeDtypeStruct((heads, 2 * rows, 128), bf16)] * 2
        + [jax.ShapeDtypeStruct((feats, 2 * rows), bf16)] * 2
        + [jax.ShapeDtypeStruct(docs.shape, jnp.int32)],
        compiler_params=small(16),
        name="expand",
    )(mine, first, last, packed, packed_other, docs)
    *pieces, docs = lax.optimization_barrier((*pieces, docs))
    pair = pl.pallas_call(
        join_kernel,
        in_specs=[SMEM_SPEC] + [VMEM_SPEC] * row_count,
        out_specs=VMEM_SPEC,
        out_shape=jax.ShapeDtypeStruct((rows, pair_feats), bf16),
        compiler_params=small(),
        name="join",
    )(place, *pieces)

    def band(name, q_panel, k_panel, block, dq, parts, q_tile, causal, q_base, outs):
        chained = dq is not None
        extra = [dq] if chained else []
        return pl.pallas_call(
            functools.partial(band_kernel, causal, q_tile, chained, len(parts), q_base),
            in_specs=[SMEM_SPEC] * 5 + [VMEM_SPEC] * (6 + len(extra) + len(parts)),
            out_specs=[VMEM_SPEC] * (1 + len(outs)),
            out_shape=[jax.ShapeDtypeStruct((2 * rows, feats), f32), *outs],
            scratch_shapes=[pltpu.VMEM((pair_feats, rows), f32)] + [pltpu.VMEM((2, rows, 128), bf16)] * 3,
            input_output_aliases={11: 0} if chained else {},
            compiler_params=small(24),
            cost_estimate=pl.CostEstimate(
                flops=20 * rows * rows * feats,
                bytes_accessed=6 << 20,
                transcendentals=2 * rows * rows * heads,
            ),
            name=name,
        )(place, q_panel, k_panel, first, last, q_ext, g_ext, q_t, g_t, docs, block, *extra, *parts)

    reach = min(chips - 1, chips // 2 + 1)
    order = [*range(2, reach + 1), 1]
    blocks = {d: up(pair, d) for d in order}
    wire = jax.ShapeDtypeStruct((pair_feats, rows), bf16)
    whole = jax.ShapeDtypeStruct((pair_feats, rows), f32)
    here = mine[:1]
    dq, own = band("own1", mine[1:], here, pair, None, [], 2 * SUB, True, 1, [whole])
    back = []
    for d in order:
        panel = (col - 2 * d).astype(jnp.int32)[None]
        q_tile = 2 * SUB if d < reach else SUB
        dq, grads = band(f"band{d}", mine, panel, blocks[d], dq, [], q_tile, False, 0, [wire])
        back.append(down(grads, d))
        if d == order[-1]:
            dq, *early = lax.optimization_barrier((dq, *back[:-1]))
    chunk = jax.ShapeDtypeStruct((pair_feats, key_rows), f32)
    parts = [own, *early, back[-1]]
    dq, *chunks = band("own0", here, here, pair, dq, parts, SUB, True, 0, [chunk] * row_count)
    chunks = [across(x, j) for j, x in enumerate(chunks)]
    other = swap(dq[rows:])
    return pl.pallas_call(
        functools.partial(finish_kernel, row_count * HEAD_DIM // key_feats, row_count),
        in_specs=[SMEM_SPEC] + [VMEM_SPEC] * (2 + row_count),
        out_specs=[VMEM_SPEC] * 3,
        out_shape=[jax.ShapeDtypeStruct((rows, feats), f32)]
        + [jax.ShapeDtypeStruct((key_rows, key_feats), f32)] * 2,
        scratch_shapes=[pltpu.VMEM((row_count, pair_feats, key_rows), f32)],
        compiler_params=small(8),
        name="finish",
    )(place, dq, *chunks, other)


def solution(mesh):
    return jax.shard_map(
        per_device,
        mesh=mesh,
        in_specs=(
            P("kcol", "qrow"),
            P(("kcol", "qrow"), None),
            P(("kcol", "qrow"), None),
            P("kcol", "qrow"),
            P("kcol", "qrow"),
            P("qrow", "kcol"),
            P(),
        ),
        out_specs=(P("kcol", "qrow"), P(("kcol", "qrow"), None), P(("kcol", "qrow"), None)),
        check_vma=False,
    )
```

```python
import functools
import jax
import jax.numpy as jnp
from jax import lax
from jax.experimental import pallas as pl
from jax.experimental.pallas import tpu as pltpu
from jax.sharding import PartitionSpec as P

HEAD_DIM = 64
GROUP = 4
DOCS = 16
FAR = 512.0
SUB = 256
EXTRA = 8
LOG2E = 1.4426950408889634
SCORE_SCALE = 0.125

f32, bf16 = jnp.float32, jnp.bfloat16
VMEM_SPEC = pl.BlockSpec(memory_space=pltpu.VMEM)
SMEM_SPEC = pl.BlockSpec(memory_space=pltpu.SMEM)


def small(mib=4):
    return pltpu.CompilerParams(vmem_limit_bytes=mib << 20)


def nt(a, b):
    return lax.dot_general(a, b, (((1,), (1,)), ((), ())), preferred_element_type=f32)


def nn(a, b):
    return lax.dot_general(a, b, (((1,), (0,)), ((), ())), preferred_element_type=f32)


def halves_swapped(x):
    return jnp.concatenate([x[:, HEAD_DIM:], x[:, :HEAD_DIM]], axis=1)


def three(x):
    high = x.astype(bf16).astype(f32)
    rest = x - high
    middle = rest.astype(bf16).astype(f32)
    return high, middle, rest - middle


def one_hot_rows(doc_row, value):
    length = doc_row.shape[1]
    ids = lax.broadcasted_iota(jnp.int32, (DOCS, length), 0).astype(f32)
    return jnp.where(ids == doc_row, value, 0.0)


def prep_kernel(place, key, value, query, grad_out, output, lse, *refs):
    pieces, packed, stage = refs[:-2], refs[-2], refs[-1]
    rows, feats = query.shape
    heads = feats // HEAD_DIM
    for r in range(len(pieces)):
        g = r * heads // GROUP
        at = slice(g * HEAD_DIM, (g + 1) * HEAD_DIM)
        stage[r] = jnp.concatenate([key[:, at], value[:, at]], axis=1)
    for j, piece in enumerate(pieces):
        piece[...] = stage[place[0] ^ j]
    packed[:, :feats] = query[...]
    packed[:, feats : 2 * feats] = grad_out[...]
    product = grad_out[...].astype(f32) * output[...].astype(f32)
    high = product.astype(bf16)
    low = (product - high.astype(f32)).astype(bf16)
    head = lax.broadcasted_iota(jnp.int32, (feats, 128), 0) // HEAD_DIM
    spot = lax.broadcasted_iota(jnp.int32, (feats, 128), 1) - EXTRA * head
    pick = jnp.where((spot >= 3) & (spot < 6), -1.0, 0.0).astype(bf16)
    d0, d1, d2 = three(nn(high, pick) + nn(low, pick))
    table = []
    for h in range(heads):
        table += list(three(-FAR - lse[h : h + 1, :])) + [jnp.zeros((EXTRA - 3, rows), f32)]
    table.append(jnp.zeros((128 - EXTRA * heads, rows), f32))
    place = lax.broadcasted_iota(jnp.int32, (rows, 128), 1) % EXTRA
    delta = jnp.where(place == 3, d0, jnp.where(place == 4, d1, d2))
    packed[:, 2 * feats :] = (jnp.concatenate(table, axis=0).T + delta).astype(bf16)


def join_kernel(place, *refs):
    parts, out = refs[:-1], refs[-1]
    length = parts[0].shape[0]
    for j, part in enumerate(parts):
        out[pl.ds(pl.multiple_of((place[0] ^ j) * length, length), length), :] = part[...]


def expand_kernel(sides, panel, first, last, *refs):
    packs, docs = refs[:sides], refs[sides]
    q_ext, g_ext, q_t, g_t = refs[sides + 1 :]
    feats = q_t.shape[0]
    heads = feats // HEAD_DIM
    rows = docs.shape[1]
    lane = lax.broadcasted_iota(jnp.int32, (rows, 128), 1)
    low_half = lane < HEAD_DIM
    source = lax.broadcasted_iota(jnp.int32, (128, 128), 0)
    target = lax.broadcasted_iota(jnp.int32, (128, 128), 1)
    offset = target % HEAD_DIM
    for side, packed in enumerate(packs):
        dst = slice(side * rows, (side + 1) * rows)
        doc_row = docs[pl.ds(panel[side], 1), :].astype(f32)
        half = [jnp.zeros((3, rows), f32), one_hot_rows(doc_row, FAR), jnp.zeros((HEAD_DIM - 3 - DOCS, rows), f32)]
        spread = jnp.concatenate(half + half, axis=0).T
        extra = packed[:, 2 * feats :]
        for p in range(heads // 2):
            at = slice(p * 128, (p + 1) * 128)
            q_pair = packed[:, at].astype(f32) * SCORE_SCALE
            g_pair = packed[:, feats + p * 128 : feats + (p + 1) * 128].astype(f32)
            q_t[at, dst] = q_pair.T.astype(bf16)
            g_t[at, dst] = g_pair.T.astype(bf16)
            base = EXTRA * jnp.where(target < HEAD_DIM, 2 * p + 1, 2 * p)
            move_q = jnp.where((source == base + offset) & (offset < 3), 1.0, 0.0).astype(bf16)
            move_g = jnp.where((source == base + 3 + offset) & (offset < 3), 1.0, 0.0).astype(bf16)
            q_more = nn(extra, move_q) + spread
            g_more = nn(extra, move_g)
            q_ext[2 * p, dst, :] = jnp.where(low_half, q_pair, q_more).astype(bf16)
            q_ext[2 * p + 1, dst, :] = jnp.where(low_half, q_more, q_pair).astype(bf16)
            g_ext[2 * p, dst, :] = jnp.where(low_half, g_pair, g_more).astype(bf16)
            g_ext[2 * p + 1, dst, :] = jnp.where(low_half, g_more, g_pair).astype(bf16)


def band_kernel(shift, q_tile, chained, *refs):
    causal = shift == 0
    q_panel, first, last, q_ext, g_ext, q_t, g_t, docs, pair = refs[:9]
    refs = refs[9 + (1 if chained else 0) :]
    dq, out, acc, k_ext, v_ext, k_lone = refs
    heads, q_rows, _ = q_ext.shape
    rows = pair.shape[0]
    subs = rows // SUB
    q_subs = q_tile // SUB
    per_panel = rows // q_tile
    q_tiles = q_panel.shape[0] * per_panel
    if not chained:
        dq[...] = jnp.zeros_like(dq)
    acc[...] = jnp.zeros_like(acc)

    def one(qt, kt, masked):
        at_q = pl.ds(pl.multiple_of(qt * q_tile, q_tile), q_tile)
        at_k = pl.ds(pl.multiple_of(kt * SUB, SUB), SUB)
        weights, score_grads = [], []
        if masked:
            ahead = (qt % per_panel) * q_tile - kt * SUB
            q_pos = lax.broadcasted_iota(jnp.int32, (q_tile, SUB), 0) + ahead
            live = lax.broadcasted_iota(jnp.int32, (q_tile, SUB), 1) <= q_pos
        for h in range(heads):
            weight = jnp.exp2(nt(q_ext[h, at_q, :], k_ext[h % 2, at_k, :]) * LOG2E)
            if masked:
                weight = jnp.where(live, weight, 0.0)
            grad = nt(g_ext[h, at_q, :], v_ext[h % 2, at_k, :])
            weights.append(weight.astype(bf16))
            score_grads.append((weight * grad).astype(bf16))
        key_sum = value_sum = 0.0
        for h in range(heads):
            at = slice(h * HEAD_DIM, (h + 1) * HEAD_DIM)
            key_sum += nn(q_t[at, at_q], score_grads[h])
            value_sum += nn(g_t[at, at_q], weights[h])
        for p in range(heads // 2):
            dq[at_q, p * 128 : (p + 1) * 128] += nn(score_grads[2 * p], k_lone[0, at_k, :]) + nn(
                score_grads[2 * p + 1], k_lone[1, at_k, :]
            )
        acc[:HEAD_DIM, at_k] += key_sum
        acc[HEAD_DIM:, at_k] += value_sum

    key_side = q_panel[0] - shift
    some = first[q_panel[0] * subs] <= last[jnp.maximum(key_side, 0) * subs + subs - 1]
    for j in range(1, q_panel.shape[0]):
        some = some | (first[q_panel[j] * subs] <= last[jnp.maximum(key_side, 0) * subs + subs - 1])
    some = some & (key_side >= 0)
    if causal:
        reach = key_side <= q_panel[0]
        for j in range(1, q_panel.shape[0]):
            reach = reach | (key_side <= q_panel[j])
        some = some & reach

    @pl.when(some)
    def _():
        lane = lax.broadcasted_iota(jnp.int32, (rows, 128), 1)
        low_half = lane < HEAD_DIM
        ones = jnp.where(lane % HEAD_DIM < 3, 1.0, 0.0)
        doc_row = docs[pl.ds(key_side, 1), :].astype(f32)
        half = [jnp.ones((3, rows), f32), one_hot_rows(doc_row, 1.0), jnp.zeros((HEAD_DIM - 3 - DOCS, rows), f32)]
        extra = jnp.concatenate(half + half, axis=0).T
        straight = pair[...].astype(f32)
        turned = halves_swapped(pair[...]).astype(f32)
        k_ext[0] = jnp.where(low_half, straight, extra).astype(bf16)
        k_ext[1] = jnp.where(low_half, extra, turned).astype(bf16)
        v_ext[0] = jnp.where(low_half, turned, ones).astype(bf16)
        v_ext[1] = jnp.where(low_half, ones, straight).astype(bf16)
        k_lone[0] = jnp.where(low_half, straight * SCORE_SCALE, 0.0).astype(bf16)
        k_lone[1] = jnp.where(low_half, 0.0, turned * SCORE_SCALE).astype(bf16)

        def step(index, carry):
            qt, kt = index // subs, index % subs
            q_at = q_panel[qt // per_panel] * subs + (qt % per_panel) * q_subs
            k_at = key_side * subs + kt
            live = first[q_at] <= last[k_at]
            if not causal:
                pl.when(live)(functools.partial(one, qt, kt, False))
            else:
                live = live & (k_at < q_at + q_subs)
                below = k_at < q_at
                pl.when(live & below)(functools.partial(one, qt, kt, False))
                pl.when(live & jnp.logical_not(below))(functools.partial(one, qt, kt, True))
            return carry

        lax.fori_loop(0, q_tiles * subs, step, 0)

    out[...] = acc[...].astype(out.dtype)


def collect_kernel(ways, place, *refs):
    parts, outs = refs[:-ways], refs[-ways:]
    chunk = outs[0].shape[1]
    for j, out in enumerate(outs):
        at = pl.ds(pl.multiple_of((place[0] ^ j) * chunk, chunk), chunk)
        total = parts[0][:, at]
        for part in parts[1:]:
            total = total + part[:, at].astype(f32)
        out[...] = total


def finish_kernel(ways, count, place, dq, *refs):
    chunks, (other,), (grad_query, grad_key, grad_value, got) = refs[:count], refs[count : count + 1], refs[count + 1 :]
    for j, chunk in enumerate(chunks):
        got[place[0] ^ j] = chunk[...]
    keys, values = [], []
    for g in range(count // ways):
        block = got[g * ways]
        for w in range(1, ways):
            block = block + got[g * ways + w]
        keys.append(block[:HEAD_DIM])
        values.append(block[HEAD_DIM:])
    grad_key[...] = jnp.concatenate(keys, axis=0).T
    grad_value[...] = jnp.concatenate(values, axis=0).T
    grad_query[...] = dq[: grad_query.shape[0], :] + other[...]


def per_device(query, key, value, output, grad_out, lse, doc_ids):
    row_count, col_count = lax.axis_size("qrow"), lax.axis_size("kcol")
    col = lax.axis_index("kcol")
    rows, feats = query.shape
    heads = feats // HEAD_DIM
    key_rows, key_feats = key.shape
    pair_feats = 2 * HEAD_DIM
    chips = col_count // 2

    def swap(x):
        return lax.ppermute(x, "kcol", [(i, i ^ 1) for i in range(col_count)])

    def up(x, d):
        return lax.ppermute(x, "kcol", [(i, i + 2 * d) for i in range(col_count - 2 * d)])

    def down(x, d):
        return lax.ppermute(x, "kcol", [(i + 2 * d, i) for i in range(col_count - 2 * d)])

    def across(x, j):
        return lax.ppermute(x, "qrow", [(i, i ^ j) for i in range(row_count)]) if j else x

    place = lax.axis_index("qrow").astype(jnp.int32)[None]
    *pieces, packed = pl.pallas_call(
        prep_kernel,
        in_specs=[SMEM_SPEC] + [VMEM_SPEC] * 6,
        out_specs=[VMEM_SPEC] * (row_count + 1),
        out_shape=[jax.ShapeDtypeStruct((key_rows, pair_feats), bf16)] * row_count
        + [jax.ShapeDtypeStruct((rows, 2 * feats + 128), bf16)],
        scratch_shapes=[pltpu.VMEM((row_count, key_rows, pair_feats), bf16)],
        compiler_params=small(56),
        name="prep",
    )(place, key, value, query, grad_out, output, lse)
    packed_other = swap(packed)
    pieces = [across(x, j) for j, x in enumerate(pieces)]

    docs = doc_ids.reshape(col_count, rows)
    first, last = docs[:, ::SUB].reshape(-1), docs[:, SUB - 1 :: SUB].reshape(-1)
    mine = jnp.stack([col, col ^ 1]).astype(jnp.int32)

    q_ext, g_ext, q_t, g_t = pl.pallas_call(
        functools.partial(expand_kernel, 2),
        in_specs=[SMEM_SPEC] * 3 + [VMEM_SPEC] * 3,
        out_specs=[VMEM_SPEC] * 4,
        out_shape=[jax.ShapeDtypeStruct((heads, 2 * rows, 128), bf16)] * 2
        + [jax.ShapeDtypeStruct((feats, 2 * rows), bf16)] * 2,
        compiler_params=small(16),
        name="expand",
    )(mine, first, last, packed, packed_other, docs)
    pair = pl.pallas_call(
        join_kernel,
        in_specs=[SMEM_SPEC] + [VMEM_SPEC] * row_count,
        out_specs=VMEM_SPEC,
        out_shape=jax.ShapeDtypeStruct((rows, pair_feats), bf16),
        compiler_params=small(),
        name="join",
    )(place, *pieces)

    def band(name, shift, block, dq, q_tile, out_type):
        chained = dq is not None
        extra = [dq] if chained else []
        return pl.pallas_call(
            functools.partial(band_kernel, shift, q_tile, chained),
            in_specs=[SMEM_SPEC] * 3 + [VMEM_SPEC] * (6 + len(extra)),
            out_specs=[VMEM_SPEC] * 2,
            out_shape=[
                jax.ShapeDtypeStruct((2 * rows, feats), f32),
                jax.ShapeDtypeStruct((pair_feats, rows), out_type),
            ],
            scratch_shapes=[pltpu.VMEM((pair_feats, rows), f32)] + [pltpu.VMEM((2, rows, 128), bf16)] * 3,
            input_output_aliases={9: 0} if chained else {},
            compiler_params=small(24),
            cost_estimate=pl.CostEstimate(
                flops=20 * rows * rows * feats,
                bytes_accessed=6 << 20,
                transcendentals=2 * rows * rows * heads,
            ),
            name=name,
        )(mine, first, last, q_ext, g_ext, q_t, g_t, docs, block, *extra)

    reach = min(chips - 1, chips // 2 + 1)
    order = [*range(2, reach + 1), 1]
    blocks = {d: up(pair, d) for d in order[:-1]}
    dq, own = band("own", 0, pair, None, SUB, f32)
    late, own = lax.optimization_barrier((pair, own))
    blocks[1] = up(late, 1)
    back = []
    for d in order:
        q_tile = 2 * SUB if d < reach else SUB
        dq, grads = band(f"band{d}", 2 * d, blocks[d], dq, q_tile, bf16)
        back.append(down(grads, d))
    dq, *back = lax.optimization_barrier((dq, *back))
    chunk = jax.ShapeDtypeStruct((pair_feats, key_rows), f32)
    chunks = pl.pallas_call(
        functools.partial(collect_kernel, row_count),
        in_specs=[SMEM_SPEC] + [VMEM_SPEC] * (1 + len(back)),
        out_specs=[VMEM_SPEC] * row_count,
        out_shape=[chunk] * row_count,
        compiler_params=small(8),
        name="collect",
    )(place, own, *back)
    chunks = [across(x, j) for j, x in enumerate(chunks)]
    other = swap(dq[rows:])
    return pl.pallas_call(
        functools.partial(finish_kernel, row_count * HEAD_DIM // key_feats, row_count),
        in_specs=[SMEM_SPEC] + [VMEM_SPEC] * (2 + row_count),
        out_specs=[VMEM_SPEC] * 3,
        out_shape=[jax.ShapeDtypeStruct((rows, feats), f32)]
        + [jax.ShapeDtypeStruct((key_rows, key_feats), f32)] * 2,
        scratch_shapes=[pltpu.VMEM((row_count, pair_feats, key_rows), f32)],
        compiler_params=small(8),
        name="finish",
    )(place, dq, *chunks, other)


def solution(mesh):
    return jax.shard_map(
        per_device,
        mesh=mesh,
        in_specs=(
            P("kcol", "qrow"),
            P(("kcol", "qrow"), None),
            P(("kcol", "qrow"), None),
            P("kcol", "qrow"),
            P("kcol", "qrow"),
            P("qrow", "kcol"),
            P(),
        ),
        out_specs=(P("kcol", "qrow"), P(("kcol", "qrow"), None), P(("kcol", "qrow"), None)),
        check_vma=False,
    )
```

```python
import functools
import jax
import jax.numpy as jnp
from jax import lax
from jax.experimental import pallas as pl
from jax.experimental.pallas import tpu as pltpu
from jax.sharding import PartitionSpec as P

HEAD_DIM = 64
GROUP = 4
DOCS = 16
FAR = 512.0
SUB = 256
EXTRA = 8
LOG2E = 1.4426950408889634
SCORE_SCALE = 0.125

f32, bf16 = jnp.float32, jnp.bfloat16
VMEM_SPEC = pl.BlockSpec(memory_space=pltpu.VMEM)
SMEM_SPEC = pl.BlockSpec(memory_space=pltpu.SMEM)


def small(mib=4):
    return pltpu.CompilerParams(vmem_limit_bytes=mib << 20)


def nt(a, b):
    return lax.dot_general(a, b, (((1,), (1,)), ((), ())), preferred_element_type=f32)


def nn(a, b):
    return lax.dot_general(a, b, (((1,), (0,)), ((), ())), preferred_element_type=f32)


def halves_swapped(x):
    return jnp.concatenate([x[:, HEAD_DIM:], x[:, :HEAD_DIM]], axis=1)


def three(x):
    high = x.astype(bf16).astype(f32)
    rest = x - high
    middle = rest.astype(bf16).astype(f32)
    return high, middle, rest - middle


def one_hot_rows(doc_row, value):
    length = doc_row.shape[1]
    ids = lax.broadcasted_iota(jnp.int32, (DOCS, length), 0).astype(f32)
    return jnp.where(ids == doc_row, value, 0.0)


def prep_kernel(place, key, value, query, grad_out, output, lse, *refs):
    pieces, packed, stage = refs[:-2], refs[-2], refs[-1]
    rows, feats = query.shape
    heads = feats // HEAD_DIM
    for r in range(len(pieces)):
        g = r * heads // GROUP
        at = slice(g * HEAD_DIM, (g + 1) * HEAD_DIM)
        stage[r] = jnp.concatenate([key[:, at], value[:, at]], axis=1)
    for j, piece in enumerate(pieces):
        piece[...] = stage[place[0] ^ j]
    packed[:, :feats] = query[...]
    packed[:, feats : 2 * feats] = grad_out[...]
    product = grad_out[...].astype(f32) * output[...].astype(f32)
    high = product.astype(bf16)
    low = (product - high.astype(f32)).astype(bf16)
    head = lax.broadcasted_iota(jnp.int32, (feats, 128), 0) // HEAD_DIM
    spot = lax.broadcasted_iota(jnp.int32, (feats, 128), 1) - EXTRA * head
    pick = jnp.where((spot >= 3) & (spot < 6), -1.0, 0.0).astype(bf16)
    d0, d1, d2 = three(nn(high, pick) + nn(low, pick))
    table = []
    for h in range(heads):
        table += list(three(-FAR - lse[h : h + 1, :])) + [jnp.zeros((EXTRA - 3, rows), f32)]
    table.append(jnp.zeros((128 - EXTRA * heads, rows), f32))
    place = lax.broadcasted_iota(jnp.int32, (rows, 128), 1) % EXTRA
    delta = jnp.where(place == 3, d0, jnp.where(place == 4, d1, d2))
    packed[:, 2 * feats :] = (jnp.concatenate(table, axis=0).T + delta).astype(bf16)


def join_kernel(place, *refs):
    parts, out = refs[:-1], refs[-1]
    length = parts[0].shape[0]
    for j, part in enumerate(parts):
        out[pl.ds(pl.multiple_of((place[0] ^ j) * length, length), length), :] = part[...]


def expand_kernel(sides, panel, first, last, *refs):
    packs, docs = refs[:sides], refs[sides]
    q_ext, g_ext, q_t, g_t, docs_out = refs[sides + 1 :]
    docs_out[...] = docs[...]
    feats = q_t.shape[0]
    heads = feats // HEAD_DIM
    rows = docs.shape[1]
    lane = lax.broadcasted_iota(jnp.int32, (rows, 128), 1)
    low_half = lane < HEAD_DIM
    source = lax.broadcasted_iota(jnp.int32, (128, 128), 0)
    target = lax.broadcasted_iota(jnp.int32, (128, 128), 1)
    offset = target % HEAD_DIM
    for side, packed in enumerate(packs):
        dst = slice(side * rows, (side + 1) * rows)
        doc_row = docs[pl.ds(panel[side], 1), :].astype(f32)
        half = [jnp.zeros((3, rows), f32), one_hot_rows(doc_row, FAR), jnp.zeros((HEAD_DIM - 3 - DOCS, rows), f32)]
        spread = jnp.concatenate(half + half, axis=0).T
        extra = packed[:, 2 * feats :]
        for p in range(heads // 2):
            at = slice(p * 128, (p + 1) * 128)
            q_pair = packed[:, at].astype(f32) * SCORE_SCALE
            g_pair = packed[:, feats + p * 128 : feats + (p + 1) * 128].astype(f32)
            q_t[at, dst] = q_pair.T.astype(bf16)
            g_t[at, dst] = g_pair.T.astype(bf16)
            base = EXTRA * jnp.where(target < HEAD_DIM, 2 * p + 1, 2 * p)
            move_q = jnp.where((source == base + offset) & (offset < 3), 1.0, 0.0).astype(bf16)
            move_g = jnp.where((source == base + 3 + offset) & (offset < 3), 1.0, 0.0).astype(bf16)
            q_more = nn(extra, move_q) + spread
            g_more = nn(extra, move_g)
            q_ext[2 * p, dst, :] = jnp.where(low_half, q_pair, q_more).astype(bf16)
            q_ext[2 * p + 1, dst, :] = jnp.where(low_half, q_more, q_pair).astype(bf16)
            g_ext[2 * p, dst, :] = jnp.where(low_half, g_pair, g_more).astype(bf16)
            g_ext[2 * p + 1, dst, :] = jnp.where(low_half, g_more, g_pair).astype(bf16)


def band_kernel(shift, q_tile, chained, *refs):
    causal = shift == 0
    q_panel, first, last, q_ext, g_ext, q_t, g_t, docs, pair = refs[:9]
    refs = refs[9 + (1 if chained else 0) :]
    dq, out, acc, k_ext, v_ext, k_lone = refs
    heads, q_rows, _ = q_ext.shape
    rows = pair.shape[0]
    subs = rows // SUB
    q_subs = q_tile // SUB
    per_panel = rows // q_tile
    q_tiles = q_panel.shape[0] * per_panel
    if not chained:
        dq[...] = jnp.zeros_like(dq)
    acc[...] = jnp.zeros_like(acc)

    def one(qt, kt, masked):
        at_q = pl.ds(pl.multiple_of(qt * q_tile, q_tile), q_tile)
        at_k = pl.ds(pl.multiple_of(kt * SUB, SUB), SUB)
        weights, score_grads = [], []
        if masked:
            ahead = (qt % per_panel) * q_tile - kt * SUB
            q_pos = lax.broadcasted_iota(jnp.int32, (q_tile, SUB), 0) + ahead
            live = lax.broadcasted_iota(jnp.int32, (q_tile, SUB), 1) <= q_pos
        for h in range(heads):
            weight = jnp.exp2(nt(q_ext[h, at_q, :], k_ext[h % 2, at_k, :]) * LOG2E)
            if masked:
                weight = jnp.where(live, weight, 0.0)
            grad = nt(g_ext[h, at_q, :], v_ext[h % 2, at_k, :])
            weights.append(weight.astype(bf16))
            score_grads.append((weight * grad).astype(bf16))
        key_sum = value_sum = 0.0
        for h in range(heads):
            at = slice(h * HEAD_DIM, (h + 1) * HEAD_DIM)
            key_sum += nn(q_t[at, at_q], score_grads[h])
            value_sum += nn(g_t[at, at_q], weights[h])
        for p in range(heads // 2):
            dq[at_q, p * 128 : (p + 1) * 128] += nn(score_grads[2 * p], k_lone[0, at_k, :]) + nn(
                score_grads[2 * p + 1], k_lone[1, at_k, :]
            )
        acc[:HEAD_DIM, at_k] += key_sum
        acc[HEAD_DIM:, at_k] += value_sum

    key_side = q_panel[0] - shift
    some = first[q_panel[0] * subs] <= last[jnp.maximum(key_side, 0) * subs + subs - 1]
    for j in range(1, q_panel.shape[0]):
        some = some | (first[q_panel[j] * subs] <= last[jnp.maximum(key_side, 0) * subs + subs - 1])
    some = some & (key_side >= 0)
    if causal:
        reach = key_side <= q_panel[0]
        for j in range(1, q_panel.shape[0]):
            reach = reach | (key_side <= q_panel[j])
        some = some & reach

    @pl.when(some)
    def _():
        lane = lax.broadcasted_iota(jnp.int32, (rows, 128), 1)
        low_half = lane < HEAD_DIM
        ones = jnp.where(lane % HEAD_DIM < 3, 1.0, 0.0)
        doc_row = docs[pl.ds(key_side, 1), :].astype(f32)
        half = [jnp.ones((3, rows), f32), one_hot_rows(doc_row, 1.0), jnp.zeros((HEAD_DIM - 3 - DOCS, rows), f32)]
        extra = jnp.concatenate(half + half, axis=0).T
        straight = pair[...].astype(f32)
        turned = halves_swapped(pair[...]).astype(f32)
        k_ext[0] = jnp.where(low_half, straight, extra).astype(bf16)
        k_ext[1] = jnp.where(low_half, extra, turned).astype(bf16)
        v_ext[0] = jnp.where(low_half, turned, ones).astype(bf16)
        v_ext[1] = jnp.where(low_half, ones, straight).astype(bf16)
        k_lone[0] = jnp.where(low_half, straight * SCORE_SCALE, 0.0).astype(bf16)
        k_lone[1] = jnp.where(low_half, 0.0, turned * SCORE_SCALE).astype(bf16)

        def step(index, carry):
            qt, kt = index // subs, index % subs
            q_at = q_panel[qt // per_panel] * subs + (qt % per_panel) * q_subs
            k_at = key_side * subs + kt
            live = first[q_at] <= last[k_at]
            if not causal:
                pl.when(live)(functools.partial(one, qt, kt, False))
            else:
                live = live & (k_at < q_at + q_subs)
                below = k_at < q_at
                pl.when(live & below)(functools.partial(one, qt, kt, False))
                pl.when(live & jnp.logical_not(below))(functools.partial(one, qt, kt, True))
            return carry

        lax.fori_loop(0, q_tiles * subs, step, 0)

    out[...] = acc[...].astype(out.dtype)


def collect_kernel(ways, place, *refs):
    parts, outs = refs[:-ways], refs[-ways:]
    chunk = outs[0].shape[1]
    for j, out in enumerate(outs):
        at = pl.ds(pl.multiple_of((place[0] ^ j) * chunk, chunk), chunk)
        total = parts[0][:, at]
        for part in parts[1:]:
            total = total + part[:, at].astype(f32)
        out[...] = total


def finish_kernel(ways, count, place, dq, *refs):
    chunks, (other,), (grad_query, grad_key, grad_value, got) = refs[:count], refs[count : count + 1], refs[count + 1 :]
    for j, chunk in enumerate(chunks):
        got[place[0] ^ j] = chunk[...]
    keys, values = [], []
    for g in range(count // ways):
        block = got[g * ways]
        for w in range(1, ways):
            block = block + got[g * ways + w]
        keys.append(block[:HEAD_DIM])
        values.append(block[HEAD_DIM:])
    grad_key[...] = jnp.concatenate(keys, axis=0).T
    grad_value[...] = jnp.concatenate(values, axis=0).T
    grad_query[...] = dq[: grad_query.shape[0], :] + other[...]


def per_device(query, key, value, output, grad_out, lse, doc_ids):
    row_count, col_count = lax.axis_size("qrow"), lax.axis_size("kcol")
    col = lax.axis_index("kcol")
    rows, feats = query.shape
    heads = feats // HEAD_DIM
    key_rows, key_feats = key.shape
    pair_feats = 2 * HEAD_DIM
    chips = col_count // 2

    def swap(x):
        return lax.ppermute(x, "kcol", [(i, i ^ 1) for i in range(col_count)])

    def up(x, d):
        return lax.ppermute(x, "kcol", [(i, i + 2 * d) for i in range(col_count - 2 * d)])

    def down(x, d):
        return lax.ppermute(x, "kcol", [(i + 2 * d, i) for i in range(col_count - 2 * d)])

    def across(x, j):
        return lax.ppermute(x, "qrow", [(i, i ^ j) for i in range(row_count)]) if j else x

    place = lax.axis_index("qrow").astype(jnp.int32)[None]
    *pieces, packed = pl.pallas_call(
        prep_kernel,
        in_specs=[SMEM_SPEC] + [VMEM_SPEC] * 6,
        out_specs=[VMEM_SPEC] * (row_count + 1),
        out_shape=[jax.ShapeDtypeStruct((key_rows, pair_feats), bf16)] * row_count
        + [jax.ShapeDtypeStruct((rows, 2 * feats + 128), bf16)],
        scratch_shapes=[pltpu.VMEM((row_count, key_rows, pair_feats), bf16)],
        compiler_params=small(56),
        name="prep",
    )(place, key, value, query, grad_out, output, lse)
    pieces = [across(x, j) for j, x in enumerate(pieces)]
    source, *pieces = lax.optimization_barrier((packed, *pieces))
    packed_other = swap(source)

    docs = doc_ids.reshape(col_count, rows)
    first, last = docs[:, ::SUB].reshape(-1), docs[:, SUB - 1 :: SUB].reshape(-1)
    mine = jnp.stack([col, col ^ 1]).astype(jnp.int32)

    q_ext, g_ext, q_t, g_t, docs = pl.pallas_call(
        functools.partial(expand_kernel, 2),
        in_specs=[SMEM_SPEC] * 3 + [VMEM_SPEC] * 3,
        out_specs=[VMEM_SPEC] * 5,
        out_shape=[jax.ShapeDtypeStruct((heads, 2 * rows, 128), bf16)] * 2
        + [jax.ShapeDtypeStruct((feats, 2 * rows), bf16)] * 2
        + [jax.ShapeDtypeStruct(docs.shape, jnp.int32)],
        compiler_params=small(16),
        name="expand",
    )(mine, first, last, packed, packed_other, docs)
    pair = pl.pallas_call(
        join_kernel,
        in_specs=[SMEM_SPEC] + [VMEM_SPEC] * row_count,
        out_specs=VMEM_SPEC,
        out_shape=jax.ShapeDtypeStruct((rows, pair_feats), bf16),
        compiler_params=small(),
        name="join",
    )(place, *pieces)

    def band(name, shift, block, dq, q_tile, out_type):
        chained = dq is not None
        extra = [dq] if chained else []
        return pl.pallas_call(
            functools.partial(band_kernel, shift, q_tile, chained),
            in_specs=[SMEM_SPEC] * 3 + [VMEM_SPEC] * (6 + len(extra)),
            out_specs=[VMEM_SPEC] * 2,
            out_shape=[
                jax.ShapeDtypeStruct((2 * rows, feats), f32),
                jax.ShapeDtypeStruct((pair_feats, rows), out_type),
            ],
            scratch_shapes=[pltpu.VMEM((pair_feats, rows), f32)] + [pltpu.VMEM((2, rows, 128), bf16)] * 3,
            input_output_aliases={9: 0} if chained else {},
            compiler_params=small(24),
            cost_estimate=pl.CostEstimate(
                flops=20 * rows * rows * feats,
                bytes_accessed=6 << 20,
                transcendentals=2 * rows * rows * heads,
            ),
            name=name,
        )(mine, first, last, q_ext, g_ext, q_t, g_t, docs, block, *extra)

    reach = min(chips - 1, chips // 2 + 1)
    blocks = {1: up(pair, 1)}
    late, docs = lax.optimization_barrier((pair, docs))
    for d in range(2, reach + 1):
        blocks[d] = up(late, d)
    dq = None
    back = []
    for d in range(1, reach + 1):
        q_tile = 2 * SUB if d < reach else SUB
        dq, grads = band(f"band{d}", 2 * d, blocks[d], dq, q_tile, bf16)
        back.append(down(grads, d))
        if d == 2:
            dq, back[0] = lax.optimization_barrier((dq, back[0]))
    dq, own = band("own", 0, pair, dq, SUB, f32)
    dq, *back = lax.optimization_barrier((dq, *back))
    chunk = jax.ShapeDtypeStruct((pair_feats, key_rows), f32)
    chunks = pl.pallas_call(
        functools.partial(collect_kernel, row_count),
        in_specs=[SMEM_SPEC] + [VMEM_SPEC] * (1 + len(back)),
        out_specs=[VMEM_SPEC] * row_count,
        out_shape=[chunk] * row_count,
        compiler_params=small(8),
        name="collect",
    )(place, own, *back)
    chunks = [across(x, j) for j, x in enumerate(chunks)]
    other = swap(dq[rows:])
    return pl.pallas_call(
        functools.partial(finish_kernel, row_count * HEAD_DIM // key_feats, row_count),
        in_specs=[SMEM_SPEC] + [VMEM_SPEC] * (2 + row_count),
        out_specs=[VMEM_SPEC] * 3,
        out_shape=[jax.ShapeDtypeStruct((rows, feats), f32)]
        + [jax.ShapeDtypeStruct((key_rows, key_feats), f32)] * 2,
        scratch_shapes=[pltpu.VMEM((row_count, pair_feats, key_rows), f32)],
        compiler_params=small(8),
        name="finish",
    )(place, dq, *chunks, other)


def solution(mesh):
    return jax.shard_map(
        per_device,
        mesh=mesh,
        in_specs=(
            P("kcol", "qrow"),
            P(("kcol", "qrow"), None),
            P(("kcol", "qrow"), None),
            P("kcol", "qrow"),
            P("kcol", "qrow"),
            P("qrow", "kcol"),
            P(),
        ),
        out_specs=(P("kcol", "qrow"), P(("kcol", "qrow"), None), P(("kcol", "qrow"), None)),
        check_vma=False,
    )
```

```python
import functools
import jax
import jax.numpy as jnp
from jax import lax
from jax.experimental import pallas as pl
from jax.experimental.pallas import tpu as pltpu
from jax.sharding import PartitionSpec as P

HEAD_DIM = 64
GROUP = 4
DOCS = 16
FAR = 512.0
SUB = 256
EXTRA = 8
PACK = 56
LOG2E = 1.4426950408889634
SCORE_SCALE = 0.125

f32, bf16 = jnp.float32, jnp.bfloat16
VMEM_SPEC = pl.BlockSpec(memory_space=pltpu.VMEM)
SMEM_SPEC = pl.BlockSpec(memory_space=pltpu.SMEM)


def small(mib=4):
    return pltpu.CompilerParams(vmem_limit_bytes=mib << 20)


def nt(a, b):
    return lax.dot_general(a, b, (((1,), (1,)), ((), ())), preferred_element_type=f32)


def nn(a, b):
    return lax.dot_general(a, b, (((1,), (0,)), ((), ())), preferred_element_type=f32)


def halves_swapped(x):
    return jnp.concatenate([x[:, HEAD_DIM:], x[:, :HEAD_DIM]], axis=1)


def three(x):
    high = x.astype(bf16).astype(f32)
    rest = x - high
    middle = rest.astype(bf16).astype(f32)
    return high, middle, rest - middle


def one_hot_rows(doc_row, value):
    length = doc_row.shape[1]
    ids = lax.broadcasted_iota(jnp.int32, (DOCS, length), 0).astype(f32)
    return jnp.where(ids == doc_row, value, 0.0)


def pack_kernel(heads, place, key, value, *refs):
    pieces, stage = refs[:-1], refs[-1]
    for r in range(len(pieces)):
        g = r * heads // GROUP
        at = slice(g * HEAD_DIM, (g + 1) * HEAD_DIM)
        stage[r] = jnp.concatenate([key[:, at], value[:, at]], axis=1)
    for j, piece in enumerate(pieces):
        piece[...] = stage[place[0] ^ j]


def prep_kernel(query, grad_out, output, lse, packed):
    rows, feats = query.shape
    heads = feats // HEAD_DIM
    packed[:, :feats] = query[...]
    packed[:, feats : 2 * feats] = grad_out[...]
    product = grad_out[...].astype(f32) * output[...].astype(f32)
    high = product.astype(bf16)
    low = (product - high.astype(f32)).astype(bf16)
    head = lax.broadcasted_iota(jnp.int32, (feats, 128), 0) // HEAD_DIM
    spot = lax.broadcasted_iota(jnp.int32, (feats, 128), 1) - EXTRA * head
    pick = jnp.where((spot >= 3) & (spot < 6), -1.0, 0.0).astype(bf16)
    d0, d1, d2 = three(nn(high, pick) + nn(low, pick))
    table = []
    for h in range(heads):
        table += list(three(-FAR - lse[h : h + 1, :])) + [jnp.zeros((EXTRA - 3, rows), f32)]
    table.append(jnp.zeros((128 - EXTRA * heads, rows), f32))
    place = lax.broadcasted_iota(jnp.int32, (rows, 128), 1) % EXTRA
    delta = jnp.where(place == 3, d0, jnp.where(place == 4, d1, d2))
    packed[:, 2 * feats :] = (jnp.concatenate(table, axis=0).T + delta).astype(bf16)


def join_kernel(place, *refs):
    parts, out = refs[:-1], refs[-1]
    length = parts[0].shape[0]
    for j, part in enumerate(parts):
        out[pl.ds(pl.multiple_of((place[0] ^ j) * length, length), length), :] = part[...]


def expand_kernel(sides, panel, first, last, *refs):
    packs, docs = refs[:sides], refs[sides]
    q_ext, g_ext, q_t, g_t, docs_out = refs[sides + 1 :]
    docs_out[...] = docs[...]
    feats = q_t.shape[0]
    heads = feats // HEAD_DIM
    rows = docs.shape[1]
    lane = lax.broadcasted_iota(jnp.int32, (rows, 128), 1)
    low_half = lane < HEAD_DIM
    source = lax.broadcasted_iota(jnp.int32, (128, 128), 0)
    target = lax.broadcasted_iota(jnp.int32, (128, 128), 1)
    offset = target % HEAD_DIM
    for side, packed in enumerate(packs):
        dst = slice(side * rows, (side + 1) * rows)
        doc_row = docs[pl.ds(panel[side], 1), :].astype(f32)
        half = [jnp.zeros((3, rows), f32), one_hot_rows(doc_row, FAR), jnp.zeros((HEAD_DIM - 3 - DOCS, rows), f32)]
        spread = jnp.concatenate(half + half, axis=0).T
        extra = packed[:, 2 * feats :]
        for p in range(heads // 2):
            at = slice(p * 128, (p + 1) * 128)
            q_pair = packed[:, at].astype(f32) * SCORE_SCALE
            g_pair = packed[:, feats + p * 128 : feats + (p + 1) * 128].astype(f32)
            q_t[at, dst] = q_pair.T.astype(bf16)
            g_t[at, dst] = g_pair.T.astype(bf16)
            base = EXTRA * jnp.where(target < HEAD_DIM, 2 * p + 1, 2 * p)
            move_q = jnp.where((source == base + offset) & (offset < 3), 1.0, 0.0).astype(bf16)
            move_g = jnp.where((source == base + 3 + offset) & (offset < 3), 1.0, 0.0).astype(bf16)
            q_more = nn(extra, move_q) + spread
            g_more = nn(extra, move_g)
            q_ext[2 * p, dst, :] = jnp.where(low_half, q_pair, q_more).astype(bf16)
            q_ext[2 * p + 1, dst, :] = jnp.where(low_half, q_more, q_pair).astype(bf16)
            g_ext[2 * p, dst, :] = jnp.where(low_half, g_pair, g_more).astype(bf16)
            g_ext[2 * p + 1, dst, :] = jnp.where(low_half, g_more, g_pair).astype(bf16)


def band_kernel(shift, q_tile, chained, *refs):
    causal = shift == 0
    q_panel, first, last, q_ext, g_ext, q_t, g_t, docs, pair = refs[:9]
    refs = refs[9 + (1 if chained else 0) :]
    dq, out, *side, acc, k_ext, v_ext, k_lone = refs
    heads, q_rows, _ = q_ext.shape
    rows = pair.shape[0]
    subs = rows // SUB
    q_subs = q_tile // SUB
    per_panel = rows // q_tile
    q_tiles = q_panel.shape[0] * per_panel
    if not chained:
        dq[...] = jnp.zeros_like(dq)
    acc[...] = jnp.zeros_like(acc)

    def one(qt, kt, masked):
        at_q = pl.ds(pl.multiple_of(qt * q_tile, q_tile), q_tile)
        at_k = pl.ds(pl.multiple_of(kt * SUB, SUB), SUB)
        weights, score_grads = [], []
        if masked:
            ahead = (qt % per_panel) * q_tile - kt * SUB
            q_pos = lax.broadcasted_iota(jnp.int32, (q_tile, SUB), 0) + ahead
            live = lax.broadcasted_iota(jnp.int32, (q_tile, SUB), 1) <= q_pos
        for h in range(heads):
            weight = jnp.exp2(nt(q_ext[h, at_q, :], k_ext[h % 2, at_k, :]) * LOG2E)
            if masked:
                weight = jnp.where(live, weight, 0.0)
            grad = nt(g_ext[h, at_q, :], v_ext[h % 2, at_k, :])
            weights.append(weight.astype(bf16))
            score_grads.append((weight * grad).astype(bf16))
        key_sum = value_sum = 0.0
        for h in range(heads):
            at = slice(h * HEAD_DIM, (h + 1) * HEAD_DIM)
            key_sum += nn(q_t[at, at_q], score_grads[h])
            value_sum += nn(g_t[at, at_q], weights[h])
        for p in range(heads // 2):
            dq[at_q, p * 128 : (p + 1) * 128] += nn(score_grads[2 * p], k_lone[0, at_k, :]) + nn(
                score_grads[2 * p + 1], k_lone[1, at_k, :]
            )
        acc[:HEAD_DIM, at_k] += key_sum
        acc[HEAD_DIM:, at_k] += value_sum

    key_side = q_panel[0] - shift
    some = first[q_panel[0] * subs] <= last[jnp.maximum(key_side, 0) * subs + subs - 1]
    for j in range(1, q_panel.shape[0]):
        some = some | (first[q_panel[j] * subs] <= last[jnp.maximum(key_side, 0) * subs + subs - 1])
    some = some & (key_side >= 0)
    if causal:
        reach = key_side <= q_panel[0]
        for j in range(1, q_panel.shape[0]):
            reach = reach | (key_side <= q_panel[j])
        some = some & reach

    @pl.when(some)
    def _():
        lane = lax.broadcasted_iota(jnp.int32, (rows, 128), 1)
        low_half = lane < HEAD_DIM
        ones = jnp.where(lane % HEAD_DIM < 3, 1.0, 0.0)
        doc_row = docs[pl.ds(key_side, 1), :].astype(f32)
        half = [jnp.ones((3, rows), f32), one_hot_rows(doc_row, 1.0), jnp.zeros((HEAD_DIM - 3 - DOCS, rows), f32)]
        extra = jnp.concatenate(half + half, axis=0).T
        straight = pair[...].astype(f32)
        turned = halves_swapped(pair[...]).astype(f32)
        k_ext[0] = jnp.where(low_half, straight, extra).astype(bf16)
        k_ext[1] = jnp.where(low_half, extra, turned).astype(bf16)
        v_ext[0] = jnp.where(low_half, turned, ones).astype(bf16)
        v_ext[1] = jnp.where(low_half, ones, straight).astype(bf16)
        k_lone[0] = jnp.where(low_half, straight * SCORE_SCALE, 0.0).astype(bf16)
        k_lone[1] = jnp.where(low_half, 0.0, turned * SCORE_SCALE).astype(bf16)

        def step(index, carry):
            qt, kt = index // subs, index % subs
            q_at = q_panel[qt // per_panel] * subs + (qt % per_panel) * q_subs
            k_at = key_side * subs + kt
            live = first[q_at] <= last[k_at]
            if not causal:
                pl.when(live)(functools.partial(one, qt, kt, False))
            else:
                live = live & (k_at < q_at + q_subs)
                below = k_at < q_at
                pl.when(live & below)(functools.partial(one, qt, kt, False))
                pl.when(live & jnp.logical_not(below))(functools.partial(one, qt, kt, True))
            return carry

        lax.fori_loop(0, q_tiles * subs, step, 0)

    out[...] = acc[...].astype(out.dtype)
    if side:
        side[0][...] = dq[rows:, :].astype(bf16)


def collect_kernel(ways, place, *refs):
    parts, outs = refs[:-ways], refs[-ways:]
    chunk = outs[0].shape[1]
    for j, out in enumerate(outs):
        at = pl.ds(pl.multiple_of((place[0] ^ j) * chunk, chunk), chunk)
        total = parts[0][:, at]
        for part in parts[1:]:
            total = total + part[:, at].astype(f32)
        out[...] = total.astype(out.dtype)


def finish_kernel(ways, count, place, dq, *refs):
    chunks, (other,), (grad_query, grad_key, grad_value, got) = refs[:count], refs[count : count + 1], refs[count + 1 :]
    for j, chunk in enumerate(chunks):
        got[place[0] ^ j] = chunk[...].astype(f32)
    keys, values = [], []
    for g in range(count // ways):
        block = got[g * ways]
        for w in range(1, ways):
            block = block + got[g * ways + w]
        keys.append(block[:HEAD_DIM])
        values.append(block[HEAD_DIM:])
    grad_key[...] = jnp.concatenate(keys, axis=0).T
    grad_value[...] = jnp.concatenate(values, axis=0).T
    grad_query[...] = dq[: grad_query.shape[0], :] + other[...].astype(f32)


def per_device(query, key, value, output, grad_out, lse, doc_ids):
    row_count, col_count = lax.axis_size("qrow"), lax.axis_size("kcol")
    col = lax.axis_index("kcol")
    rows, feats = query.shape
    heads = feats // HEAD_DIM
    key_rows, key_feats = key.shape
    pair_feats = 2 * HEAD_DIM
    chips = col_count // 2

    def swap(x):
        return lax.ppermute(x, "kcol", [(i, i ^ 1) for i in range(col_count)])

    def up(x, d):
        return lax.ppermute(x, "kcol", [(i, i + 2 * d) for i in range(col_count - 2 * d)])

    def down(x, d):
        return lax.ppermute(x, "kcol", [(i + 2 * d, i) for i in range(col_count - 2 * d)])

    def across(x, j):
        return lax.ppermute(x, "qrow", [(i, i ^ j) for i in range(row_count)]) if j else x

    place = lax.axis_index("qrow").astype(jnp.int32)[None]
    pieces = pl.pallas_call(
        functools.partial(pack_kernel, heads),
        in_specs=[SMEM_SPEC] + [VMEM_SPEC] * 2,
        out_specs=[VMEM_SPEC] * row_count,
        out_shape=[jax.ShapeDtypeStruct((key_rows, pair_feats), bf16)] * row_count,
        scratch_shapes=[pltpu.VMEM((row_count, key_rows, pair_feats), bf16)],
        compiler_params=small(PACK),
        name="pack",
    )(place, key, value)
    packed = pl.pallas_call(
        prep_kernel,
        in_specs=[VMEM_SPEC] * 4,
        out_specs=VMEM_SPEC,
        out_shape=jax.ShapeDtypeStruct((rows, 2 * feats + 128), bf16),
        compiler_params=small(56),
        name="prep",
    )(query, grad_out, output, lse)
    pieces = [across(x, j) for j, x in enumerate(pieces)]
    source, *pieces = lax.optimization_barrier((packed, *pieces))
    packed_other = swap(source)

    docs = doc_ids.reshape(col_count, rows)
    first, last = docs[:, ::SUB].reshape(-1), docs[:, SUB - 1 :: SUB].reshape(-1)
    mine = jnp.stack([col, col ^ 1]).astype(jnp.int32)

    q_ext, g_ext, q_t, g_t, docs = pl.pallas_call(
        functools.partial(expand_kernel, 2),
        in_specs=[SMEM_SPEC] * 3 + [VMEM_SPEC] * 3,
        out_specs=[VMEM_SPEC] * 5,
        out_shape=[jax.ShapeDtypeStruct((heads, 2 * rows, 128), bf16)] * 2
        + [jax.ShapeDtypeStruct((feats, 2 * rows), bf16)] * 2
        + [jax.ShapeDtypeStruct(docs.shape, jnp.int32)],
        compiler_params=small(16),
        name="expand",
    )(mine, first, last, packed, packed_other, docs)
    pair = pl.pallas_call(
        join_kernel,
        in_specs=[SMEM_SPEC] + [VMEM_SPEC] * row_count,
        out_specs=VMEM_SPEC,
        out_shape=jax.ShapeDtypeStruct((rows, pair_feats), bf16),
        compiler_params=small(),
        name="join",
    )(place, *pieces)

    def band(name, shift, block, dq, q_tile, out_type):
        chained = dq is not None
        extra = [dq] if chained else []
        return pl.pallas_call(
            functools.partial(band_kernel, shift, q_tile, chained),
            in_specs=[SMEM_SPEC] * 3 + [VMEM_SPEC] * (6 + len(extra)),
            out_specs=[VMEM_SPEC] * (2 if shift else 3),
            out_shape=[
                jax.ShapeDtypeStruct((2 * rows, feats), f32),
                jax.ShapeDtypeStruct((pair_feats, rows), out_type),
            ]
            + ([] if shift else [jax.ShapeDtypeStruct((rows, feats), bf16)]),
            scratch_shapes=[pltpu.VMEM((pair_feats, rows), f32)] + [pltpu.VMEM((2, rows, 128), bf16)] * 3,
            input_output_aliases={9: 0} if chained else {},
            compiler_params=small(24),
            cost_estimate=pl.CostEstimate(
                flops=20 * rows * rows * feats,
                bytes_accessed=6 << 20,
                transcendentals=2 * rows * rows * heads,
            ),
            name=name,
        )(mine, first, last, q_ext, g_ext, q_t, g_t, docs, block, *extra)

    reach = min(chips - 1, chips // 2 + 1)
    blocks = {1: up(pair, 1)}
    late, docs = lax.optimization_barrier((pair, docs))
    for d in range(2, reach + 1):
        blocks[d] = up(late, d)
    dq = None
    back = []
    for d in range(1, reach + 1):
        q_tile = 2 * SUB if d < reach else SUB
        dq, grads = band(f"band{d}", 2 * d, blocks[d], dq, q_tile, bf16)
        back.append(down(grads, d))
        if d == 1 and reach > 1:
            dq, *later = lax.optimization_barrier((dq, *[blocks[e] for e in range(2, reach + 1)]))
            blocks.update(zip(range(2, reach + 1), later))
        if d == 2:
            dq, back[0] = lax.optimization_barrier((dq, back[0]))
    if reach > 1:
        dq, *back[1:-1] = lax.optimization_barrier((dq, *back[1:-1]))
    dq, own, side = band("own", 0, pair, dq, SUB, f32)
    side, *back = lax.optimization_barrier((side, *back))
    chunk = jax.ShapeDtypeStruct((pair_feats, key_rows), bf16)
    chunks = pl.pallas_call(
        functools.partial(collect_kernel, row_count),
        in_specs=[SMEM_SPEC] + [VMEM_SPEC] * (1 + len(back)),
        out_specs=[VMEM_SPEC] * row_count,
        out_shape=[chunk] * row_count,
        compiler_params=small(8),
        name="collect",
    )(place, own, *back)
    chunks = [across(x, j) for j, x in enumerate(chunks)]
    other = swap(side)
    return pl.pallas_call(
        functools.partial(finish_kernel, row_count * HEAD_DIM // key_feats, row_count),
        in_specs=[SMEM_SPEC] + [VMEM_SPEC] * (2 + row_count),
        out_specs=[VMEM_SPEC] * 3,
        out_shape=[jax.ShapeDtypeStruct((rows, feats), f32)]
        + [jax.ShapeDtypeStruct((key_rows, key_feats), f32)] * 2,
        scratch_shapes=[pltpu.VMEM((row_count, pair_feats, key_rows), f32)],
        compiler_params=small(8),
        name="finish",
    )(place, dq, *chunks, other)


def solution(mesh):
    return jax.shard_map(
        per_device,
        mesh=mesh,
        in_specs=(
            P("kcol", "qrow"),
            P(("kcol", "qrow"), None),
            P(("kcol", "qrow"), None),
            P("kcol", "qrow"),
            P("kcol", "qrow"),
            P("qrow", "kcol"),
            P(),
        ),
        out_specs=(P("kcol", "qrow"), P(("kcol", "qrow"), None), P(("kcol", "qrow"), None)),
        check_vma=False,
    )
```

```python
import functools
import jax
import jax.numpy as jnp
from jax import lax
from jax.experimental import pallas as pl
from jax.experimental.pallas import tpu as pltpu
from jax.sharding import PartitionSpec as P

HEAD_DIM = 64
GROUP = 4
DOCS = 16
FAR = 512.0
SUB = 256
EXTRA = 8
PACK = 56
LOG2E = 1.4426950408889634
SCORE_SCALE = 0.125

f32, bf16 = jnp.float32, jnp.bfloat16
VMEM_SPEC = pl.BlockSpec(memory_space=pltpu.VMEM)
SMEM_SPEC = pl.BlockSpec(memory_space=pltpu.SMEM)


def small(mib=4):
    return pltpu.CompilerParams(vmem_limit_bytes=mib << 20)


def nt(a, b):
    return lax.dot_general(a, b, (((1,), (1,)), ((), ())), preferred_element_type=f32)


def nn(a, b):
    return lax.dot_general(a, b, (((1,), (0,)), ((), ())), preferred_element_type=f32)


def halves_swapped(x):
    return jnp.concatenate([x[:, HEAD_DIM:], x[:, :HEAD_DIM]], axis=1)


def three(x):
    high = x.astype(bf16).astype(f32)
    rest = x - high
    middle = rest.astype(bf16).astype(f32)
    return high, middle, rest - middle


def one_hot_rows(doc_row, value):
    length = doc_row.shape[1]
    ids = lax.broadcasted_iota(jnp.int32, (DOCS, length), 0).astype(f32)
    return jnp.where(ids == doc_row, value, 0.0)


def pack_kernel(heads, place, key, value, *refs):
    pieces, stage = refs[:-1], refs[-1]
    for r in range(len(pieces)):
        g = r * heads // GROUP
        at = slice(g * HEAD_DIM, (g + 1) * HEAD_DIM)
        stage[r] = jnp.concatenate([key[:, at], value[:, at]], axis=1)
    for j, piece in enumerate(pieces):
        piece[...] = stage[place[0] ^ j]


def prep_kernel(query, grad_out, output, lse, packed):
    rows, feats = query.shape
    heads = feats // HEAD_DIM
    packed[:, :feats] = query[...]
    packed[:, feats : 2 * feats] = grad_out[...]
    product = grad_out[...].astype(f32) * output[...].astype(f32)
    high = product.astype(bf16)
    low = (product - high.astype(f32)).astype(bf16)
    head = lax.broadcasted_iota(jnp.int32, (feats, 128), 0) // HEAD_DIM
    spot = lax.broadcasted_iota(jnp.int32, (feats, 128), 1) - EXTRA * head
    pick = jnp.where((spot >= 3) & (spot < 6), -1.0, 0.0).astype(bf16)
    d0, d1, d2 = three(nn(high, pick) + nn(low, pick))
    table = []
    for h in range(heads):
        table += list(three(-FAR - lse[h : h + 1, :])) + [jnp.zeros((EXTRA - 3, rows), f32)]
    table.append(jnp.zeros((128 - EXTRA * heads, rows), f32))
    place = lax.broadcasted_iota(jnp.int32, (rows, 128), 1) % EXTRA
    delta = jnp.where(place == 3, d0, jnp.where(place == 4, d1, d2))
    packed[:, 2 * feats :] = (jnp.concatenate(table, axis=0).T + delta).astype(bf16)


def join_kernel(place, *refs):
    parts, out = refs[:-1], refs[-1]
    length = parts[0].shape[0]
    for j, part in enumerate(parts):
        out[pl.ds(pl.multiple_of((place[0] ^ j) * length, length), length), :] = part[...]


def expand_kernel(sides, panel, first, last, *refs):
    packs, docs = refs[:sides], refs[sides]
    q_ext, g_ext, q_t, g_t, docs_out = refs[sides + 1 :]
    docs_out[...] = docs[...]
    feats = q_t.shape[0]
    heads = feats // HEAD_DIM
    rows = docs.shape[1]
    lane = lax.broadcasted_iota(jnp.int32, (rows, 128), 1)
    low_half = lane < HEAD_DIM
    source = lax.broadcasted_iota(jnp.int32, (128, 128), 0)
    target = lax.broadcasted_iota(jnp.int32, (128, 128), 1)
    offset = target % HEAD_DIM
    for side, packed in enumerate(packs):
        dst = slice(side * rows, (side + 1) * rows)
        doc_row = docs[pl.ds(panel[side], 1), :].astype(f32)
        half = [jnp.zeros((3, rows), f32), one_hot_rows(doc_row, FAR), jnp.zeros((HEAD_DIM - 3 - DOCS, rows), f32)]
        spread = jnp.concatenate(half + half, axis=0).T
        extra = packed[:, 2 * feats :]
        for p in range(heads // 2):
            at = slice(p * 128, (p + 1) * 128)
            q_pair = packed[:, at].astype(f32) * SCORE_SCALE
            g_pair = packed[:, feats + p * 128 : feats + (p + 1) * 128].astype(f32)
            q_t[at, dst] = q_pair.T.astype(bf16)
            g_t[at, dst] = g_pair.T.astype(bf16)
            base = EXTRA * jnp.where(target < HEAD_DIM, 2 * p + 1, 2 * p)
            move_q = jnp.where((source == base + offset) & (offset < 3), 1.0, 0.0).astype(bf16)
            move_g = jnp.where((source == base + 3 + offset) & (offset < 3), 1.0, 0.0).astype(bf16)
            q_more = nn(extra, move_q) + spread
            g_more = nn(extra, move_g)
            q_ext[2 * p, dst, :] = jnp.where(low_half, q_pair, q_more).astype(bf16)
            q_ext[2 * p + 1, dst, :] = jnp.where(low_half, q_more, q_pair).astype(bf16)
            g_ext[2 * p, dst, :] = jnp.where(low_half, g_pair, g_more).astype(bf16)
            g_ext[2 * p + 1, dst, :] = jnp.where(low_half, g_more, g_pair).astype(bf16)


def band_kernel(shift, q_tile, chained, *refs):
    causal = shift == 0
    q_panel, first, last, q_ext, g_ext, q_t, g_t, docs, pair = refs[:9]
    refs = refs[9 + (1 if chained else 0) :]
    dq, out, *side, acc, k_ext, v_ext, k_lone = refs
    heads, q_rows, _ = q_ext.shape
    rows = pair.shape[0]
    subs = rows // SUB
    q_subs = q_tile // SUB
    per_panel = rows // q_tile
    q_tiles = q_panel.shape[0] * per_panel
    if not chained:
        dq[...] = jnp.zeros_like(dq)
    acc[...] = jnp.zeros_like(acc)

    def one(qt, kt, masked):
        at_q = pl.ds(pl.multiple_of(qt * q_tile, q_tile), q_tile)
        at_k = pl.ds(pl.multiple_of(kt * SUB, SUB), SUB)
        weights, score_grads = [], []
        if masked:
            ahead = (qt % per_panel) * q_tile - kt * SUB
            q_pos = lax.broadcasted_iota(jnp.int32, (q_tile, SUB), 0) + ahead
            live = lax.broadcasted_iota(jnp.int32, (q_tile, SUB), 1) <= q_pos
        for h in range(heads):
            weight = jnp.exp2(nt(q_ext[h, at_q, :], k_ext[h % 2, at_k, :]) * LOG2E)
            if masked:
                weight = jnp.where(live, weight, 0.0)
            grad = nt(g_ext[h, at_q, :], v_ext[h % 2, at_k, :])
            weights.append(weight.astype(bf16))
            score_grads.append((weight * grad).astype(bf16))
        key_sum = value_sum = 0.0
        for h in range(heads):
            at = slice(h * HEAD_DIM, (h + 1) * HEAD_DIM)
            key_sum += nn(q_t[at, at_q], score_grads[h])
            value_sum += nn(g_t[at, at_q], weights[h])
        for p in range(heads // 2):
            dq[at_q, p * 128 : (p + 1) * 128] += nn(score_grads[2 * p], k_lone[0, at_k, :]) + nn(
                score_grads[2 * p + 1], k_lone[1, at_k, :]
            )
        acc[:HEAD_DIM, at_k] += key_sum
        acc[HEAD_DIM:, at_k] += value_sum

    key_side = q_panel[0] - shift
    some = first[q_panel[0] * subs] <= last[jnp.maximum(key_side, 0) * subs + subs - 1]
    for j in range(1, q_panel.shape[0]):
        some = some | (first[q_panel[j] * subs] <= last[jnp.maximum(key_side, 0) * subs + subs - 1])
    some = some & (key_side >= 0)
    if causal:
        reach = key_side <= q_panel[0]
        for j in range(1, q_panel.shape[0]):
            reach = reach | (key_side <= q_panel[j])
        some = some & reach

    @pl.when(some)
    def _():
        lane = lax.broadcasted_iota(jnp.int32, (rows, 128), 1)
        low_half = lane < HEAD_DIM
        ones = jnp.where(lane % HEAD_DIM < 3, 1.0, 0.0)
        doc_row = docs[pl.ds(key_side, 1), :].astype(f32)
        half = [jnp.ones((3, rows), f32), one_hot_rows(doc_row, 1.0), jnp.zeros((HEAD_DIM - 3 - DOCS, rows), f32)]
        extra = jnp.concatenate(half + half, axis=0).T
        straight = pair[...].astype(f32)
        turned = halves_swapped(pair[...]).astype(f32)
        k_ext[0] = jnp.where(low_half, straight, extra).astype(bf16)
        k_ext[1] = jnp.where(low_half, extra, turned).astype(bf16)
        v_ext[0] = jnp.where(low_half, turned, ones).astype(bf16)
        v_ext[1] = jnp.where(low_half, ones, straight).astype(bf16)
        k_lone[0] = jnp.where(low_half, straight * SCORE_SCALE, 0.0).astype(bf16)
        k_lone[1] = jnp.where(low_half, 0.0, turned * SCORE_SCALE).astype(bf16)

        def step(index, carry):
            qt, kt = index // subs, index % subs
            q_at = q_panel[qt // per_panel] * subs + (qt % per_panel) * q_subs
            k_at = key_side * subs + kt
            live = first[q_at] <= last[k_at]
            if not causal:
                pl.when(live)(functools.partial(one, qt, kt, False))
            else:
                live = live & (k_at < q_at + q_subs)
                below = k_at < q_at
                pl.when(live & below)(functools.partial(one, qt, kt, False))
                pl.when(live & jnp.logical_not(below))(functools.partial(one, qt, kt, True))
            return carry

        lax.fori_loop(0, q_tiles * subs, step, 0)

    out[...] = acc[...].astype(out.dtype)
    if side:
        side[0][...] = dq[rows:, :].astype(bf16)


def collect_kernel(ways, place, *refs):
    parts, outs = refs[:-ways], refs[-ways:]
    chunk = outs[0].shape[1]
    for j, out in enumerate(outs):
        at = pl.ds(pl.multiple_of((place[0] ^ j) * chunk, chunk), chunk)
        total = parts[0][:, at]
        for part in parts[1:]:
            total = total + part[:, at].astype(f32)
        out[...] = total.astype(out.dtype)


def finish_kernel(ways, count, place, dq, *refs):
    chunks, (other,), (grad_query, grad_key, grad_value, got) = refs[:count], refs[count : count + 1], refs[count + 1 :]
    for j, chunk in enumerate(chunks):
        got[place[0] ^ j] = chunk[...].astype(f32)
    keys, values = [], []
    for g in range(count // ways):
        block = got[g * ways]
        for w in range(1, ways):
            block = block + got[g * ways + w]
        keys.append(block[:HEAD_DIM])
        values.append(block[HEAD_DIM:])
    grad_key[...] = jnp.concatenate(keys, axis=0).T
    grad_value[...] = jnp.concatenate(values, axis=0).T
    grad_query[...] = dq[: grad_query.shape[0], :] + other[...].astype(f32)


def per_device(query, key, value, output, grad_out, lse, doc_ids):
    row_count, col_count = lax.axis_size("qrow"), lax.axis_size("kcol")
    col = lax.axis_index("kcol")
    rows, feats = query.shape
    heads = feats // HEAD_DIM
    key_rows, key_feats = key.shape
    pair_feats = 2 * HEAD_DIM
    chips = col_count // 2

    def swap(x):
        return lax.ppermute(x, "kcol", [(i, i ^ 1) for i in range(col_count)])

    def up(x, d):
        return lax.ppermute(x, "kcol", [(i, i + 2 * d) for i in range(col_count - 2 * d)])

    def down(x, d):
        return lax.ppermute(x, "kcol", [(i + 2 * d, i) for i in range(col_count - 2 * d)])

    def across(x, j):
        return lax.ppermute(x, "qrow", [(i, i ^ j) for i in range(row_count)]) if j else x

    place = lax.axis_index("qrow").astype(jnp.int32)[None]
    pieces = pl.pallas_call(
        functools.partial(pack_kernel, heads),
        in_specs=[SMEM_SPEC] + [VMEM_SPEC] * 2,
        out_specs=[VMEM_SPEC] * row_count,
        out_shape=[jax.ShapeDtypeStruct((key_rows, pair_feats), bf16)] * row_count,
        scratch_shapes=[pltpu.VMEM((row_count, key_rows, pair_feats), bf16)],
        compiler_params=small(PACK),
        name="pack",
    )(place, key, value)
    packed = pl.pallas_call(
        prep_kernel,
        in_specs=[VMEM_SPEC] * 4,
        out_specs=VMEM_SPEC,
        out_shape=jax.ShapeDtypeStruct((rows, 2 * feats + 128), bf16),
        compiler_params=small(56),
        name="prep",
    )(query, grad_out, output, lse)
    pieces = [across(x, j) for j, x in enumerate(pieces)]
    source, *pieces = lax.optimization_barrier((packed, *pieces))
    packed_other = swap(source)

    docs = doc_ids.reshape(col_count, rows)
    first, last = docs[:, ::SUB].reshape(-1), docs[:, SUB - 1 :: SUB].reshape(-1)
    mine = jnp.stack([col, col ^ 1]).astype(jnp.int32)

    q_ext, g_ext, q_t, g_t, docs = pl.pallas_call(
        functools.partial(expand_kernel, 2),
        in_specs=[SMEM_SPEC] * 3 + [VMEM_SPEC] * 3,
        out_specs=[VMEM_SPEC] * 5,
        out_shape=[jax.ShapeDtypeStruct((heads, 2 * rows, 128), bf16)] * 2
        + [jax.ShapeDtypeStruct((feats, 2 * rows), bf16)] * 2
        + [jax.ShapeDtypeStruct(docs.shape, jnp.int32)],
        compiler_params=small(16),
        name="expand",
    )(mine, first, last, packed, packed_other, docs)
    pair = pl.pallas_call(
        join_kernel,
        in_specs=[SMEM_SPEC] + [VMEM_SPEC] * row_count,
        out_specs=VMEM_SPEC,
        out_shape=jax.ShapeDtypeStruct((rows, pair_feats), bf16),
        compiler_params=small(),
        name="join",
    )(place, *pieces)

    def band(name, shift, block, dq, q_tile, out_type):
        chained = dq is not None
        extra = [dq] if chained else []
        return pl.pallas_call(
            functools.partial(band_kernel, shift, q_tile, chained),
            in_specs=[SMEM_SPEC] * 3 + [VMEM_SPEC] * (6 + len(extra)),
            out_specs=[VMEM_SPEC] * (3 if shift == 2 else 2),
            out_shape=[
                jax.ShapeDtypeStruct((2 * rows, feats), f32),
                jax.ShapeDtypeStruct((pair_feats, rows), out_type),
            ]
            + ([jax.ShapeDtypeStruct((rows, feats), bf16)] if shift == 2 else []),
            scratch_shapes=[pltpu.VMEM((pair_feats, rows), f32)] + [pltpu.VMEM((2, rows, 128), bf16)] * 3,
            input_output_aliases={9: 0} if chained else {},
            compiler_params=small(24),
            cost_estimate=pl.CostEstimate(
                flops=20 * rows * rows * feats,
                bytes_accessed=6 << 20,
                transcendentals=2 * rows * rows * heads,
            ),
            name=name,
        )(mine, first, last, q_ext, g_ext, q_t, g_t, docs, block, *extra)

    reach = min(chips - 1, chips // 2 + 1)
    order = [*range(2, reach + 1), 1]
    blocks = {d: up(pair, d) for d in order[:-1]}
    dq, own = band("own", 0, pair, None, SUB, f32)
    late, own = lax.optimization_barrier((pair, own))
    blocks[1] = up(late, 1)
    back = []
    for d in order[:-1]:
        dq, grads = band(f"band{d}", 2 * d, blocks[d], dq, 2 * SUB if d < reach else SUB, bf16)
        back.append(down(grads, d))
    dq, grads, side = band("band1", 2, blocks[1], dq, 2 * SUB, bf16)
    back.append(down(grads, 1))
    side, *back = lax.optimization_barrier((side, *back))
    chunk = jax.ShapeDtypeStruct((pair_feats, key_rows), bf16)
    chunks = pl.pallas_call(
        functools.partial(collect_kernel, row_count),
        in_specs=[SMEM_SPEC] + [VMEM_SPEC] * (1 + len(back)),
        out_specs=[VMEM_SPEC] * row_count,
        out_shape=[chunk] * row_count,
        compiler_params=small(8),
        name="collect",
    )(place, own, *back)
    chunks = [across(x, j) for j, x in enumerate(chunks)]
    other = swap(side)
    return pl.pallas_call(
        functools.partial(finish_kernel, row_count * HEAD_DIM // key_feats, row_count),
        in_specs=[SMEM_SPEC] + [VMEM_SPEC] * (2 + row_count),
        out_specs=[VMEM_SPEC] * 3,
        out_shape=[jax.ShapeDtypeStruct((rows, feats), f32)]
        + [jax.ShapeDtypeStruct((key_rows, key_feats), f32)] * 2,
        scratch_shapes=[pltpu.VMEM((row_count, pair_feats, key_rows), f32)],
        compiler_params=small(8),
        name="finish",
    )(place, dq, *chunks, other)


def solution(mesh):
    return jax.shard_map(
        per_device,
        mesh=mesh,
        in_specs=(
            P("kcol", "qrow"),
            P(("kcol", "qrow"), None),
            P(("kcol", "qrow"), None),
            P("kcol", "qrow"),
            P("kcol", "qrow"),
            P("qrow", "kcol"),
            P(),
        ),
        out_specs=(P("kcol", "qrow"), P(("kcol", "qrow"), None), P(("kcol", "qrow"), None)),
        check_vma=False,
    )
```

```python
import functools
import jax
import jax.numpy as jnp
from jax import lax
from jax.experimental import pallas as pl
from jax.experimental.pallas import tpu as pltpu
from jax.sharding import PartitionSpec as P

HEAD_DIM = 64
GROUP = 4
DOCS = 16
FAR = 512.0
SUB = 256
EXTRA = 8
PACK = 56
LOG2E = 1.4426950408889634
SCORE_SCALE = 0.125

f32, bf16 = jnp.float32, jnp.bfloat16
VMEM_SPEC = pl.BlockSpec(memory_space=pltpu.VMEM)
SMEM_SPEC = pl.BlockSpec(memory_space=pltpu.SMEM)


def small(mib=4):
    return pltpu.CompilerParams(vmem_limit_bytes=mib << 20)


def nt(a, b):
    return lax.dot_general(a, b, (((1,), (1,)), ((), ())), preferred_element_type=f32)


def nn(a, b):
    return lax.dot_general(a, b, (((1,), (0,)), ((), ())), preferred_element_type=f32)


def halves_swapped(x):
    return jnp.concatenate([x[:, HEAD_DIM:], x[:, :HEAD_DIM]], axis=1)


def three(x):
    high = x.astype(bf16).astype(f32)
    rest = x - high
    middle = rest.astype(bf16).astype(f32)
    return high, middle, rest - middle


def one_hot_rows(doc_row, value):
    length = doc_row.shape[1]
    ids = lax.broadcasted_iota(jnp.int32, (DOCS, length), 0).astype(f32)
    return jnp.where(ids == doc_row, value, 0.0)


def pack_kernel(heads, place, key, value, *refs):
    pieces, stage = refs[:-1], refs[-1]
    for r in range(len(pieces)):
        g = r * heads // GROUP
        at = slice(g * HEAD_DIM, (g + 1) * HEAD_DIM)
        stage[r] = jnp.concatenate([key[:, at], value[:, at]], axis=1)
    for j, piece in enumerate(pieces):
        piece[...] = stage[place[0] ^ j]


def prep_kernel(query, grad_out, output, lse, packed):
    rows, feats = query.shape
    heads = feats // HEAD_DIM
    packed[:, :feats] = query[...]
    packed[:, feats : 2 * feats] = grad_out[...]
    product = grad_out[...].astype(f32) * output[...].astype(f32)
    high = product.astype(bf16)
    low = (product - high.astype(f32)).astype(bf16)
    head = lax.broadcasted_iota(jnp.int32, (feats, 128), 0) // HEAD_DIM
    spot = lax.broadcasted_iota(jnp.int32, (feats, 128), 1) - EXTRA * head
    pick = jnp.where((spot >= 3) & (spot < 6), -1.0, 0.0).astype(bf16)
    d0, d1, d2 = three(nn(high, pick) + nn(low, pick))
    table = []
    for h in range(heads):
        table += list(three(-FAR - lse[h : h + 1, :])) + [jnp.zeros((EXTRA - 3, rows), f32)]
    table.append(jnp.zeros((128 - EXTRA * heads, rows), f32))
    place = lax.broadcasted_iota(jnp.int32, (rows, 128), 1) % EXTRA
    delta = jnp.where(place == 3, d0, jnp.where(place == 4, d1, d2))
    packed[:, 2 * feats :] = (jnp.concatenate(table, axis=0).T + delta).astype(bf16)


def join_kernel(place, *refs):
    parts, out = refs[:-1], refs[-1]
    length = parts[0].shape[0]
    for j, part in enumerate(parts):
        out[pl.ds(pl.multiple_of((place[0] ^ j) * length, length), length), :] = part[...]


def expand_kernel(sides, panel, first, last, *refs):
    packs, docs = refs[:sides], refs[sides]
    q_ext, g_ext, q_t, g_t, docs_out = refs[sides + 1 :]
    docs_out[...] = docs[...]
    feats = q_t.shape[0]
    heads = feats // HEAD_DIM
    rows = docs.shape[1]
    lane = lax.broadcasted_iota(jnp.int32, (rows, 128), 1)
    low_half = lane < HEAD_DIM
    source = lax.broadcasted_iota(jnp.int32, (128, 128), 0)
    target = lax.broadcasted_iota(jnp.int32, (128, 128), 1)
    offset = target % HEAD_DIM
    for side, packed in enumerate(packs):
        dst = slice(side * rows, (side + 1) * rows)
        doc_row = docs[pl.ds(panel[side], 1), :].astype(f32)
        half = [jnp.zeros((3, rows), f32), one_hot_rows(doc_row, FAR), jnp.zeros((HEAD_DIM - 3 - DOCS, rows), f32)]
        spread = jnp.concatenate(half + half, axis=0).T
        extra = packed[:, 2 * feats :]
        for p in range(heads // 2):
            at = slice(p * 128, (p + 1) * 128)
            q_pair = packed[:, at].astype(f32) * SCORE_SCALE
            g_pair = packed[:, feats + p * 128 : feats + (p + 1) * 128].astype(f32)
            q_t[at, dst] = q_pair.T.astype(bf16)
            g_t[at, dst] = g_pair.T.astype(bf16)
            base = EXTRA * jnp.where(target < HEAD_DIM, 2 * p + 1, 2 * p)
            move_q = jnp.where((source == base + offset) & (offset < 3), 1.0, 0.0).astype(bf16)
            move_g = jnp.where((source == base + 3 + offset) & (offset < 3), 1.0, 0.0).astype(bf16)
            q_more = nn(extra, move_q) + spread
            g_more = nn(extra, move_g)
            q_ext[2 * p, dst, :] = jnp.where(low_half, q_pair, q_more).astype(bf16)
            q_ext[2 * p + 1, dst, :] = jnp.where(low_half, q_more, q_pair).astype(bf16)
            g_ext[2 * p, dst, :] = jnp.where(low_half, g_pair, g_more).astype(bf16)
            g_ext[2 * p + 1, dst, :] = jnp.where(low_half, g_more, g_pair).astype(bf16)


def band_kernel(shift, q_tile, chained, only, *refs):
    causal = shift == 0
    q_panel, first, last, q_ext, g_ext, q_t, g_t, docs, pair = refs[:9]
    refs = refs[9 + (1 if chained else 0) :]
    dq, out, *side, acc, k_ext, v_ext, k_lone = refs
    heads, q_rows, _ = q_ext.shape
    rows = pair.shape[0]
    subs = rows // SUB
    q_subs = q_tile // SUB
    per_panel = rows // q_tile
    sides = range(2) if only is None else [only]
    q_start, q_tiles = sides[0] * per_panel, len(sides) * per_panel
    if not chained:
        dq[...] = jnp.zeros_like(dq)
    acc[...] = jnp.zeros_like(acc)

    def one(qt, kt, masked, width=SUB):
        at_q = pl.ds(pl.multiple_of(qt * q_tile, q_tile), q_tile)
        at_k = pl.ds(pl.multiple_of(kt * SUB, SUB), width)
        weights, score_grads = [], []
        if masked:
            ahead = (qt % per_panel) * q_tile - kt * SUB
            q_pos = lax.broadcasted_iota(jnp.int32, (q_tile, SUB), 0) + ahead
            live = lax.broadcasted_iota(jnp.int32, (q_tile, SUB), 1) <= q_pos
        scores = [nt(q_ext[h, at_q, :], k_ext[h % 2, at_k, :]) for h in range(heads)]
        grads = [nt(g_ext[h, at_q, :], v_ext[h % 2, at_k, :]) for h in range(heads)]
        for score, grad in zip(scores, grads):
            weight = jnp.exp2(score * LOG2E)
            if masked:
                weight = jnp.where(live, weight, 0.0)
            weights.append(weight.astype(bf16))
            score_grads.append((weight * grad).astype(bf16))
        key_sum = value_sum = 0.0
        for h in range(heads):
            at = slice(h * HEAD_DIM, (h + 1) * HEAD_DIM)
            key_sum += nn(q_t[at, at_q], score_grads[h])
            value_sum += nn(g_t[at, at_q], weights[h])
        for p in range(heads // 2):
            dq[at_q, p * 128 : (p + 1) * 128] += nn(score_grads[2 * p], k_lone[0, at_k, :]) + nn(
                score_grads[2 * p + 1], k_lone[1, at_k, :]
            )
        acc[:HEAD_DIM, at_k] += key_sum
        acc[HEAD_DIM:, at_k] += value_sum

    key_side = q_panel[0] - shift
    key_end = last[jnp.maximum(key_side, 0) * subs + subs - 1]
    some = False
    for j in sides:
        some = some | ((first[q_panel[j] * subs] <= key_end) & (key_side <= q_panel[j]))
    some = some & (key_side >= 0)

    @pl.when(some)
    def _():
        lane = lax.broadcasted_iota(jnp.int32, (rows, 128), 1)
        low_half = lane < HEAD_DIM
        ones = jnp.where(lane % HEAD_DIM < 3, 1.0, 0.0)
        doc_row = docs[pl.ds(key_side, 1), :].astype(f32)
        half = [jnp.ones((3, rows), f32), one_hot_rows(doc_row, 1.0), jnp.zeros((HEAD_DIM - 3 - DOCS, rows), f32)]
        extra = jnp.concatenate(half + half, axis=0).T
        straight = pair[...].astype(f32)
        turned = halves_swapped(pair[...]).astype(f32)
        k_ext[0] = jnp.where(low_half, straight, extra).astype(bf16)
        k_ext[1] = jnp.where(low_half, extra, turned).astype(bf16)
        v_ext[0] = jnp.where(low_half, turned, ones).astype(bf16)
        v_ext[1] = jnp.where(low_half, ones, straight).astype(bf16)
        k_lone[0] = jnp.where(low_half, straight * SCORE_SCALE, 0.0).astype(bf16)
        k_lone[1] = jnp.where(low_half, 0.0, turned * SCORE_SCALE).astype(bf16)

        def step(index, carry):
            qt, kt = q_start + index // subs, index % subs
            q_at = q_panel[qt // per_panel] * subs + (qt % per_panel) * q_subs
            k_at = key_side * subs + kt
            live = first[q_at] <= last[k_at]
            if not causal:
                pl.when(live)(functools.partial(one, qt, kt, False))
            else:
                live = live & (k_at < q_at + q_subs)
                below = k_at < q_at
                pl.when(live & below)(functools.partial(one, qt, kt, False))
                pl.when(live & jnp.logical_not(below))(functools.partial(one, qt, kt, True))
            return carry

        def wide(index, carry):
            qt, kt = q_start + index // (subs // 2), 2 * (index % (subs // 2))
            q_at = q_panel[qt // per_panel] * subs + (qt % per_panel) * q_subs
            k_at = key_side * subs + kt
            both = first[q_at] <= last[k_at]
            after = jnp.logical_not(both) & (first[q_at] <= last[k_at + 1])
            pl.when(both)(functools.partial(one, qt, kt, False, 2 * SUB))
            pl.when(after)(functools.partial(one, qt, kt + 1, False))
            return carry

        if causal or q_subs == 1 or subs % 2:
            lax.fori_loop(0, q_tiles * subs, step, 0)
        else:
            lax.fori_loop(0, q_tiles * subs // 2, wide, 0)

    out[...] = acc[...].astype(out.dtype)
    if side:
        side[0][...] = dq[rows:, :].astype(bf16)


def collect_kernel(ways, place, *refs):
    parts, outs = refs[:-ways], refs[-ways:]
    chunk = outs[0].shape[1]
    for j, out in enumerate(outs):
        at = pl.ds(pl.multiple_of((place[0] ^ j) * chunk, chunk), chunk)
        total = parts[0][:, at]
        for part in parts[1:]:
            total = total + part[:, at].astype(f32)
        out[...] = total.astype(out.dtype)


def finish_kernel(ways, count, place, dq, *refs):
    chunks, (other,), (grad_query, grad_key, grad_value, got) = refs[:count], refs[count : count + 1], refs[count + 1 :]
    for j, chunk in enumerate(chunks):
        got[place[0] ^ j] = chunk[...].astype(f32)
    keys, values = [], []
    for g in range(count // ways):
        block = got[g * ways]
        for w in range(1, ways):
            block = block + got[g * ways + w]
        keys.append(block[:HEAD_DIM])
        values.append(block[HEAD_DIM:])
    grad_key[...] = jnp.concatenate(keys, axis=0).T
    grad_value[...] = jnp.concatenate(values, axis=0).T
    grad_query[...] = dq[: grad_query.shape[0], :] + other[...].astype(f32)


def per_device(query, key, value, output, grad_out, lse, doc_ids):
    row_count, col_count = lax.axis_size("qrow"), lax.axis_size("kcol")
    col = lax.axis_index("kcol")
    rows, feats = query.shape
    heads = feats // HEAD_DIM
    key_rows, key_feats = key.shape
    pair_feats = 2 * HEAD_DIM
    chips = col_count // 2

    def swap(x):
        return lax.ppermute(x, "kcol", [(i, i ^ 1) for i in range(col_count)])

    def up(x, d):
        return lax.ppermute(x, "kcol", [(i, (i + 2 * d) % col_count) for i in range(col_count)])

    def down(x, d):
        return lax.ppermute(x, "kcol", [(i + 2 * d, i) for i in range(col_count - 2 * d)])

    def across(x, j):
        return lax.ppermute(x, "qrow", [(i, i ^ j) for i in range(row_count)]) if j else x

    place = lax.axis_index("qrow").astype(jnp.int32)[None]
    pieces = pl.pallas_call(
        functools.partial(pack_kernel, heads),
        in_specs=[SMEM_SPEC] + [VMEM_SPEC] * 2,
        out_specs=[VMEM_SPEC] * row_count,
        out_shape=[jax.ShapeDtypeStruct((key_rows, pair_feats), bf16)] * row_count,
        scratch_shapes=[pltpu.VMEM((row_count, key_rows, pair_feats), bf16)],
        compiler_params=small(PACK),
        name="pack",
    )(place, key, value)
    packed = pl.pallas_call(
        prep_kernel,
        in_specs=[VMEM_SPEC] * 4,
        out_specs=VMEM_SPEC,
        out_shape=jax.ShapeDtypeStruct((rows, 2 * feats + 128), bf16),
        compiler_params=small(56),
        name="prep",
    )(query, grad_out, output, lse)
    pieces = [across(x, j) for j, x in enumerate(pieces)]
    source, *pieces = lax.optimization_barrier((packed, *pieces))
    packed_other = swap(source)

    docs = doc_ids.reshape(col_count, rows)
    first, last = docs[:, ::SUB].reshape(-1), docs[:, SUB - 1 :: SUB].reshape(-1)
    mine = jnp.stack([col, col ^ 1]).astype(jnp.int32)

    q_ext, g_ext, q_t, g_t, docs = pl.pallas_call(
        functools.partial(expand_kernel, 2),
        in_specs=[SMEM_SPEC] * 3 + [VMEM_SPEC] * 3,
        out_specs=[VMEM_SPEC] * 5,
        out_shape=[jax.ShapeDtypeStruct((heads, 2 * rows, 128), bf16)] * 2
        + [jax.ShapeDtypeStruct((feats, 2 * rows), bf16)] * 2
        + [jax.ShapeDtypeStruct(docs.shape, jnp.int32)],
        compiler_params=small(16),
        name="expand",
    )(mine, first, last, packed, packed_other, docs)
    pair = pl.pallas_call(
        join_kernel,
        in_specs=[SMEM_SPEC] + [VMEM_SPEC] * row_count,
        out_specs=VMEM_SPEC,
        out_shape=jax.ShapeDtypeStruct((rows, pair_feats), bf16),
        compiler_params=small(),
        name="join",
    )(place, *pieces)

    def band(name, shift, block, dq, q_tile, side=None):
        chained = dq is not None
        extra = [dq] if chained else []
        return pl.pallas_call(
            functools.partial(band_kernel, shift, q_tile, chained, side),
            in_specs=[SMEM_SPEC] * 3 + [VMEM_SPEC] * (6 + len(extra)),
            out_specs=[VMEM_SPEC] * (3 if side == 1 else 2),
            out_shape=[
                jax.ShapeDtypeStruct((2 * rows, feats), f32),
                jax.ShapeDtypeStruct((pair_feats, rows), f32 if shift == 0 else bf16),
            ]
            + ([jax.ShapeDtypeStruct((rows, feats), bf16)] if side == 1 else []),
            scratch_shapes=[pltpu.VMEM((pair_feats, rows), f32)] + [pltpu.VMEM((2, rows, 128), bf16)] * 3,
            input_output_aliases={9: 0} if chained else {},
            compiler_params=small(24),
            cost_estimate=pl.CostEstimate(
                flops=20 * rows * rows * feats,
                bytes_accessed=6 << 20,
                transcendentals=2 * rows * rows * heads,
            ),
            name=name,
        )(mine, first, last, q_ext, g_ext, q_t, g_t, docs, block, *extra)

    reach = min(chips - 1, chips // 2 + 1)
    order = [*range(2, reach + 1), 1]
    blocks = {d: up(pair, d) for d in order[:-1]}
    dq, own = band("own", 0, pair, None, SUB, 0)
    late, own = lax.optimization_barrier((pair, own))
    blocks[1] = up(late, 1)
    back = []
    for d in order:
        dq, grads = band(f"band{d}", 2 * d, blocks[d], dq, 2 * SUB if d < reach else SUB)
        back.append(down(grads, d))
    if reach > 1:
        dq, back[-2] = lax.optimization_barrier((dq, back[-2]))
    dq, more, side = band("rest", 0, pair, dq, 2 * SUB, 1)
    side, more, *back = lax.optimization_barrier((side, more, *back))
    chunk = jax.ShapeDtypeStruct((pair_feats, key_rows), bf16)
    chunks = pl.pallas_call(
        functools.partial(collect_kernel, row_count),
        in_specs=[SMEM_SPEC] + [VMEM_SPEC] * (2 + len(back)),
        out_specs=[VMEM_SPEC] * row_count,
        out_shape=[chunk] * row_count,
        compiler_params=small(8),
        name="collect",
    )(place, own, more, *back)
    chunks = [across(x, j) for j, x in enumerate(chunks)]
    other = swap(side)
    return pl.pallas_call(
        functools.partial(finish_kernel, row_count * HEAD_DIM // key_feats, row_count),
        in_specs=[SMEM_SPEC] + [VMEM_SPEC] * (2 + row_count),
        out_specs=[VMEM_SPEC] * 3,
        out_shape=[jax.ShapeDtypeStruct((rows, feats), f32)]
        + [jax.ShapeDtypeStruct((key_rows, key_feats), f32)] * 2,
        scratch_shapes=[pltpu.VMEM((row_count, pair_feats, key_rows), f32)],
        compiler_params=small(8),
        name="finish",
    )(place, dq, *chunks, other)


def solution(mesh):
    return jax.shard_map(
        per_device,
        mesh=mesh,
        in_specs=(
            P("kcol", "qrow"),
            P(("kcol", "qrow"), None),
            P(("kcol", "qrow"), None),
            P("kcol", "qrow"),
            P("kcol", "qrow"),
            P("qrow", "kcol"),
            P(),
        ),
        out_specs=(P("kcol", "qrow"), P(("kcol", "qrow"), None), P(("kcol", "qrow"), None)),
        check_vma=False,
    )
```

```python
import functools
import jax
import jax.numpy as jnp
from jax import lax
from jax.experimental import pallas as pl
from jax.experimental.pallas import tpu as pltpu
from jax.sharding import PartitionSpec as P

HEAD_DIM = 64
GROUP = 4
DOCS = 16
FAR = 512.0
SUB = 256
EXTRA = 8
PACK = 56
LOG2E = 1.4426950408889634
SCORE_SCALE = 0.125

f32, bf16 = jnp.float32, jnp.bfloat16
VMEM_SPEC = pl.BlockSpec(memory_space=pltpu.VMEM)
SMEM_SPEC = pl.BlockSpec(memory_space=pltpu.SMEM)


def small(mib=4):
    return pltpu.CompilerParams(vmem_limit_bytes=mib << 20)


def nt(a, b):
    return lax.dot_general(a, b, (((1,), (1,)), ((), ())), preferred_element_type=f32)


def nn(a, b):
    return lax.dot_general(a, b, (((1,), (0,)), ((), ())), preferred_element_type=f32)


def halves_swapped(x):
    return jnp.concatenate([x[:, HEAD_DIM:], x[:, :HEAD_DIM]], axis=1)


def three(x):
    high = x.astype(bf16).astype(f32)
    rest = x - high
    middle = rest.astype(bf16).astype(f32)
    return high, middle, rest - middle


def one_hot_rows(doc_row, value):
    length = doc_row.shape[1]
    ids = lax.broadcasted_iota(jnp.int32, (DOCS, length), 0).astype(f32)
    return jnp.where(ids == doc_row, value, 0.0)


def pack_kernel(heads, place, key, value, *refs):
    pieces, stage = refs[:-1], refs[-1]
    for r in range(len(pieces)):
        g = r * heads // GROUP
        at = slice(g * HEAD_DIM, (g + 1) * HEAD_DIM)
        stage[r] = jnp.concatenate([key[:, at], value[:, at]], axis=1)
    for j, piece in enumerate(pieces):
        piece[...] = stage[place[0] ^ j]


def prep_kernel(query, grad_out, output, lse, packed):
    rows, feats = query.shape
    heads = feats // HEAD_DIM
    packed[:, :feats] = query[...]
    packed[:, feats : 2 * feats] = grad_out[...]
    product = grad_out[...].astype(f32) * output[...].astype(f32)
    high = product.astype(bf16)
    low = (product - high.astype(f32)).astype(bf16)
    head = lax.broadcasted_iota(jnp.int32, (feats, 128), 0) // HEAD_DIM
    spot = lax.broadcasted_iota(jnp.int32, (feats, 128), 1) - EXTRA * head
    pick = jnp.where((spot >= 3) & (spot < 6), -1.0, 0.0).astype(bf16)
    d0, d1, d2 = three(nn(high, pick) + nn(low, pick))
    table = []
    for h in range(heads):
        table += list(three(-FAR - lse[h : h + 1, :])) + [jnp.zeros((EXTRA - 3, rows), f32)]
    table.append(jnp.zeros((128 - EXTRA * heads, rows), f32))
    place = lax.broadcasted_iota(jnp.int32, (rows, 128), 1) % EXTRA
    delta = jnp.where(place == 3, d0, jnp.where(place == 4, d1, d2))
    packed[:, 2 * feats :] = (jnp.concatenate(table, axis=0).T + delta).astype(bf16)


def join_kernel(place, *refs):
    parts, out = refs[:-1], refs[-1]
    length = parts[0].shape[0]
    for j, part in enumerate(parts):
        out[pl.ds(pl.multiple_of((place[0] ^ j) * length, length), length), :] = part[...]


def expand_kernel(sides, panel, first, last, *refs):
    packs, docs = refs[:sides], refs[sides]
    q_ext, g_ext, q_t, g_t, docs_out = refs[sides + 1 :]
    docs_out[...] = docs[...]
    feats = q_t.shape[0]
    heads = feats // HEAD_DIM
    rows = docs.shape[1]
    lane = lax.broadcasted_iota(jnp.int32, (rows, 128), 1)
    low_half = lane < HEAD_DIM
    source = lax.broadcasted_iota(jnp.int32, (128, 128), 0)
    target = lax.broadcasted_iota(jnp.int32, (128, 128), 1)
    offset = target % HEAD_DIM
    for side, packed in enumerate(packs):
        dst = slice(side * rows, (side + 1) * rows)
        doc_row = docs[pl.ds(panel[side], 1), :].astype(f32)
        half = [jnp.zeros((3, rows), f32), one_hot_rows(doc_row, FAR), jnp.zeros((HEAD_DIM - 3 - DOCS, rows), f32)]
        spread = jnp.concatenate(half + half, axis=0).T
        extra = packed[:, 2 * feats :]
        for p in range(heads // 2):
            at = slice(p * 128, (p + 1) * 128)
            q_pair = packed[:, at].astype(f32) * SCORE_SCALE
            g_pair = packed[:, feats + p * 128 : feats + (p + 1) * 128].astype(f32)
            q_t[at, dst] = q_pair.T.astype(bf16)
            g_t[at, dst] = g_pair.T.astype(bf16)
            base = EXTRA * jnp.where(target < HEAD_DIM, 2 * p + 1, 2 * p)
            move_q = jnp.where((source == base + offset) & (offset < 3), 1.0, 0.0).astype(bf16)
            move_g = jnp.where((source == base + 3 + offset) & (offset < 3), 1.0, 0.0).astype(bf16)
            q_more = nn(extra, move_q) + spread
            g_more = nn(extra, move_g)
            q_ext[2 * p, dst, :] = jnp.where(low_half, q_pair, q_more).astype(bf16)
            q_ext[2 * p + 1, dst, :] = jnp.where(low_half, q_more, q_pair).astype(bf16)
            g_ext[2 * p, dst, :] = jnp.where(low_half, g_pair, g_more).astype(bf16)
            g_ext[2 * p + 1, dst, :] = jnp.where(low_half, g_more, g_pair).astype(bf16)


def band_kernel(shifts, q_tiles_by, chained, only, *refs):
    count = len(shifts)
    q_panel, first, last, q_ext, g_ext, q_t, g_t, docs = refs[:8]
    pairs = refs[8 : 8 + count]
    refs = refs[8 + count + (1 if chained else 0) :]
    dq, outs, refs = refs[0], refs[1 : 1 + count], refs[1 + count :]
    *side, acc, k_ext, v_ext, k_lone = refs
    if not chained:
        dq[...] = jnp.zeros_like(dq)
    operands = (q_panel, first, last, q_ext, g_ext, q_t, g_t, docs)
    for shift, q_tile, pair, out in zip(shifts, q_tiles_by, pairs, outs):
        one_band(shift, q_tile, only, operands, pair, dq, out, acc, k_ext, v_ext, k_lone)
    if side:
        side[0][...] = dq[pairs[0].shape[0] :, :].astype(bf16)


def one_band(shift, q_tile, only, operands, pair, dq, out, acc, k_ext, v_ext, k_lone):
    causal = shift == 0
    q_panel, first, last, q_ext, g_ext, q_t, g_t, docs = operands
    heads, q_rows, _ = q_ext.shape
    rows = pair.shape[0]
    subs = rows // SUB
    q_subs = q_tile // SUB
    per_panel = rows // q_tile
    sides = range(2) if only is None else [only]
    q_start, q_tiles = sides[0] * per_panel, len(sides) * per_panel
    acc[...] = jnp.zeros_like(acc)

    def one(qt, kt, masked, width=SUB):
        at_q = pl.ds(pl.multiple_of(qt * q_tile, q_tile), q_tile)
        at_k = pl.ds(pl.multiple_of(kt * SUB, SUB), width)
        weights, score_grads = [], []
        if masked:
            ahead = (qt % per_panel) * q_tile - kt * SUB
            q_pos = lax.broadcasted_iota(jnp.int32, (q_tile, SUB), 0) + ahead
            live = lax.broadcasted_iota(jnp.int32, (q_tile, SUB), 1) <= q_pos
        scores = [nt(q_ext[h, at_q, :], k_ext[h % 2, at_k, :]) for h in range(heads)]
        grads = [nt(g_ext[h, at_q, :], v_ext[h % 2, at_k, :]) for h in range(heads)]
        for score, grad in zip(scores, grads):
            weight = jnp.exp2(score * LOG2E)
            if masked:
                weight = jnp.where(live, weight, 0.0)
            weights.append(weight.astype(bf16))
            score_grads.append((weight * grad).astype(bf16))
        key_sum = value_sum = 0.0
        for h in range(heads):
            at = slice(h * HEAD_DIM, (h + 1) * HEAD_DIM)
            key_sum += nn(q_t[at, at_q], score_grads[h])
            value_sum += nn(g_t[at, at_q], weights[h])
        for p in range(heads // 2):
            dq[at_q, p * 128 : (p + 1) * 128] += nn(score_grads[2 * p], k_lone[0, at_k, :]) + nn(
                score_grads[2 * p + 1], k_lone[1, at_k, :]
            )
        acc[:HEAD_DIM, at_k] += key_sum
        acc[HEAD_DIM:, at_k] += value_sum

    key_side = q_panel[0] - shift
    key_end = last[jnp.maximum(key_side, 0) * subs + subs - 1]
    some = False
    for j in sides:
        some = some | ((first[q_panel[j] * subs] <= key_end) & (key_side <= q_panel[j]))
    some = some & (key_side >= 0)

    @pl.when(some)
    def _():
        lane = lax.broadcasted_iota(jnp.int32, (rows, 128), 1)
        low_half = lane < HEAD_DIM
        ones = jnp.where(lane % HEAD_DIM < 3, 1.0, 0.0)
        doc_row = docs[pl.ds(key_side, 1), :].astype(f32)
        half = [jnp.ones((3, rows), f32), one_hot_rows(doc_row, 1.0), jnp.zeros((HEAD_DIM - 3 - DOCS, rows), f32)]
        extra = jnp.concatenate(half + half, axis=0).T
        straight = pair[...].astype(f32)
        turned = halves_swapped(pair[...]).astype(f32)
        k_ext[0] = jnp.where(low_half, straight, extra).astype(bf16)
        k_ext[1] = jnp.where(low_half, extra, turned).astype(bf16)
        v_ext[0] = jnp.where(low_half, turned, ones).astype(bf16)
        v_ext[1] = jnp.where(low_half, ones, straight).astype(bf16)
        k_lone[0] = jnp.where(low_half, straight * SCORE_SCALE, 0.0).astype(bf16)
        k_lone[1] = jnp.where(low_half, 0.0, turned * SCORE_SCALE).astype(bf16)

        def step(index, carry):
            qt, kt = q_start + index // subs, index % subs
            q_at = q_panel[qt // per_panel] * subs + (qt % per_panel) * q_subs
            k_at = key_side * subs + kt
            live = first[q_at] <= last[k_at]
            if not causal:
                pl.when(live)(functools.partial(one, qt, kt, False))
            else:
                live = live & (k_at < q_at + q_subs)
                below = k_at < q_at
                pl.when(live & below)(functools.partial(one, qt, kt, False))
                pl.when(live & jnp.logical_not(below))(functools.partial(one, qt, kt, True))
            return carry

        def wide(index, carry):
            qt, kt = q_start + index // (subs // 2), 2 * (index % (subs // 2))
            q_at = q_panel[qt // per_panel] * subs + (qt % per_panel) * q_subs
            k_at = key_side * subs + kt
            both = first[q_at] <= last[k_at]
            after = jnp.logical_not(both) & (first[q_at] <= last[k_at + 1])
            pl.when(both)(functools.partial(one, qt, kt, False, 2 * SUB))
            pl.when(after)(functools.partial(one, qt, kt + 1, False))
            return carry

        if causal or q_subs == 1 or subs % 2:
            lax.fori_loop(0, q_tiles * subs, step, 0)
        else:
            lax.fori_loop(0, q_tiles * subs // 2, wide, 0)

    out[...] = acc[...].astype(out.dtype)


def collect_kernel(ways, place, *refs):
    parts, outs = refs[:-ways], refs[-ways:]
    chunk = outs[0].shape[1]
    for j, out in enumerate(outs):
        at = pl.ds(pl.multiple_of((place[0] ^ j) * chunk, chunk), chunk)
        total = parts[0][:, at]
        for part in parts[1:]:
            total = total + part[:, at].astype(f32)
        out[...] = total.astype(out.dtype)


def finish_kernel(ways, count, place, dq, *refs):
    chunks, (other,), (grad_query, grad_key, grad_value, got) = refs[:count], refs[count : count + 1], refs[count + 1 :]
    for j, chunk in enumerate(chunks):
        got[place[0] ^ j] = chunk[...].astype(f32)
    keys, values = [], []
    for g in range(count // ways):
        block = got[g * ways]
        for w in range(1, ways):
            block = block + got[g * ways + w]
        keys.append(block[:HEAD_DIM])
        values.append(block[HEAD_DIM:])
    grad_key[...] = jnp.concatenate(keys, axis=0).T
    grad_value[...] = jnp.concatenate(values, axis=0).T
    grad_query[...] = dq[: grad_query.shape[0], :] + other[...].astype(f32)


def per_device(query, key, value, output, grad_out, lse, doc_ids):
    row_count, col_count = lax.axis_size("qrow"), lax.axis_size("kcol")
    col = lax.axis_index("kcol")
    rows, feats = query.shape
    heads = feats // HEAD_DIM
    key_rows, key_feats = key.shape
    pair_feats = 2 * HEAD_DIM
    chips = col_count // 2

    def swap(x):
        return lax.ppermute(x, "kcol", [(i, i ^ 1) for i in range(col_count)])

    def up(x, d):
        return lax.ppermute(x, "kcol", [(i, (i + 2 * d) % col_count) for i in range(col_count)])

    def down(x, d):
        return lax.ppermute(x, "kcol", [(i + 2 * d, i) for i in range(col_count - 2 * d)])

    def across(x, j):
        return lax.ppermute(x, "qrow", [(i, i ^ j) for i in range(row_count)]) if j else x

    place = lax.axis_index("qrow").astype(jnp.int32)[None]
    pieces = pl.pallas_call(
        functools.partial(pack_kernel, heads),
        in_specs=[SMEM_SPEC] + [VMEM_SPEC] * 2,
        out_specs=[VMEM_SPEC] * row_count,
        out_shape=[jax.ShapeDtypeStruct((key_rows, pair_feats), bf16)] * row_count,
        scratch_shapes=[pltpu.VMEM((row_count, key_rows, pair_feats), bf16)],
        compiler_params=small(PACK),
        name="pack",
    )(place, key, value)
    packed = pl.pallas_call(
        prep_kernel,
        in_specs=[VMEM_SPEC] * 4,
        out_specs=VMEM_SPEC,
        out_shape=jax.ShapeDtypeStruct((rows, 2 * feats + 128), bf16),
        compiler_params=small(56),
        name="prep",
    )(query, grad_out, output, lse)
    pieces = [across(x, j) for j, x in enumerate(pieces)]
    source, *pieces = lax.optimization_barrier((packed, *pieces))
    packed_other = swap(source)

    docs = doc_ids.reshape(col_count, rows)
    first, last = docs[:, ::SUB].reshape(-1), docs[:, SUB - 1 :: SUB].reshape(-1)
    mine = jnp.stack([col, col ^ 1]).astype(jnp.int32)

    q_ext, g_ext, q_t, g_t, docs = pl.pallas_call(
        functools.partial(expand_kernel, 2),
        in_specs=[SMEM_SPEC] * 3 + [VMEM_SPEC] * 3,
        out_specs=[VMEM_SPEC] * 5,
        out_shape=[jax.ShapeDtypeStruct((heads, 2 * rows, 128), bf16)] * 2
        + [jax.ShapeDtypeStruct((feats, 2 * rows), bf16)] * 2
        + [jax.ShapeDtypeStruct(docs.shape, jnp.int32)],
        compiler_params=small(16),
        name="expand",
    )(mine, first, last, packed, packed_other, docs)
    pair = pl.pallas_call(
        join_kernel,
        in_specs=[SMEM_SPEC] + [VMEM_SPEC] * row_count,
        out_specs=VMEM_SPEC,
        out_shape=jax.ShapeDtypeStruct((rows, pair_feats), bf16),
        compiler_params=small(),
        name="join",
    )(place, *pieces)

    def band(name, shifts, held, dq, q_sizes, side=None):
        chained = dq is not None
        extra = [dq] if chained else []
        count = len(shifts)
        return pl.pallas_call(
            functools.partial(band_kernel, shifts, q_sizes, chained, side),
            in_specs=[SMEM_SPEC] * 3 + [VMEM_SPEC] * (5 + count + len(extra)),
            out_specs=[VMEM_SPEC] * (1 + count + (1 if side == 1 else 0)),
            out_shape=[jax.ShapeDtypeStruct((2 * rows, feats), f32)]
            + [jax.ShapeDtypeStruct((pair_feats, rows), bf16 if x else f32) for x in shifts]
            + ([jax.ShapeDtypeStruct((rows, feats), bf16)] if side == 1 else []),
            scratch_shapes=[pltpu.VMEM((pair_feats, rows), f32)] + [pltpu.VMEM((2, rows, 128), bf16)] * 3,
            input_output_aliases={8 + count: 0} if chained else {},
            compiler_params=small(24),
            cost_estimate=pl.CostEstimate(
                flops=20 * rows * rows * feats * count,
                bytes_accessed=6 << 20,
                transcendentals=2 * rows * rows * heads * count,
            ),
            name=name,
        )(mine, first, last, q_ext, g_ext, q_t, g_t, docs, *held, *extra)

    reach = min(chips - 1, chips // 2 + 1)
    order = [*range(2, reach + 1), 1]
    blocks = {d: up(pair, d) for d in order[:-1]}
    dq, own = band("own", [0], [pair], None, [SUB], 0)
    late, own = lax.optimization_barrier((pair, own))
    blocks[1] = up(late, 1)
    back = []
    sizes = {d: 2 * SUB if d < reach else SUB for d in order}
    if reach > 1:
        far = order[:-1]
        dq, *grads = band(
            "far", [2 * d for d in far], [blocks[d] for d in far], dq, [sizes[d] for d in far]
        )
        back += [down(x, d) for x, d in zip(grads, far)]
    dq, grads = band("near", [2], [blocks[1]], dq, [sizes[1]])
    back.append(down(grads, 1))
    if reach > 1:
        dq, back[-2] = lax.optimization_barrier((dq, back[-2]))
    dq, more, side = band("rest", [0], [pair], dq, [2 * SUB], 1)
    side, more, *back = lax.optimization_barrier((side, more, *back))
    chunk = jax.ShapeDtypeStruct((pair_feats, key_rows), bf16)
    chunks = pl.pallas_call(
        functools.partial(collect_kernel, row_count),
        in_specs=[SMEM_SPEC] + [VMEM_SPEC] * (2 + len(back)),
        out_specs=[VMEM_SPEC] * row_count,
        out_shape=[chunk] * row_count,
        compiler_params=small(8),
        name="collect",
    )(place, own, more, *back)
    chunks = [across(x, j) for j, x in enumerate(chunks)]
    other = swap(side)
    return pl.pallas_call(
        functools.partial(finish_kernel, row_count * HEAD_DIM // key_feats, row_count),
        in_specs=[SMEM_SPEC] + [VMEM_SPEC] * (2 + row_count),
        out_specs=[VMEM_SPEC] * 3,
        out_shape=[jax.ShapeDtypeStruct((rows, feats), f32)]
        + [jax.ShapeDtypeStruct((key_rows, key_feats), f32)] * 2,
        scratch_shapes=[pltpu.VMEM((row_count, pair_feats, key_rows), f32)],
        compiler_params=small(8),
        name="finish",
    )(place, dq, *chunks, other)


def solution(mesh):
    return jax.shard_map(
        per_device,
        mesh=mesh,
        in_specs=(
            P("kcol", "qrow"),
            P(("kcol", "qrow"), None),
            P(("kcol", "qrow"), None),
            P("kcol", "qrow"),
            P("kcol", "qrow"),
            P("qrow", "kcol"),
            P(),
        ),
        out_specs=(P("kcol", "qrow"), P(("kcol", "qrow"), None), P(("kcol", "qrow"), None)),
        check_vma=False,
    )
```
